32 devices in a mesh: date: 4 (over y, x), tile: 8 (over z, core).
Axes of the slice: x: 2, y: 2, z: 4, core: 2. Of those that a mesh axis runs over, the one named last changes fastest.
Arguments:
- swath_intensities: bfloat16 [4, 128, 64, 2, 512], P('date', 'tile'), may hold values from 0.0099487305 to 1
- destination_patch: int32 [128, 1], P('tile'), may hold values from 0 to 7; in each aligned block of 16 rows (0 to 15, 16 to 31, ...) at most 4 rows name the same one
- swath_leading_scanline: int32 [128], P('tile'), may hold values from 0 to 64
- receiver_floor_intensity: float32 [4, 1024, 2, 512], P('date', 'tile'), may hold values from 0.1 to 1
Outputs:
- filtered: bfloat16 [4, 1024, 2, 512], P('date', 'tile')
The draws below stay inside these ranges and needn't reach their ends.
Inputs may be any that keep to these rules, and one draw needn't show every extreme that they name: `destination_patch`: among the 16 blocks of one device no owner is named more than 4 times.
All inputs are finite; a program needn't handle non-finite values.
Results may differ from the reference program's by a relative error of at most 0.008.
Values may be sent and summed in bfloat16 or wider, within the bound.
No kernel may reach another device: no remote copies, remote signals or barrier semaphores. Data moves between devices by JAX's collectives and lax.ppermute only.
A program may use at most 128 MiB of HBM per device.

```python
import math
import jax
import jax.numpy as jnp
import numpy as np
from jax import lax

RASTER_BREADTH = 512
SWATH_HEIGHT = 64
PATCH_HEIGHT = 128
SWATHS_HELD = 16
SHIPMENT_BOUND = 4
SWATHS_ALTOGETHER = 128
PASSES_ALTOGETHER = 4
N_TILE = 8


def touch_ends(array, stream_key, smallest, high):
    index_at = [jax.random.randint(jax.random.fold_in(stream_key, axis), (), 0, length) for axis, length in enumerate(array.shape)]
    longest = array.shape.index(max(array.shape))
    next_to = index_at[:longest] + [(index_at[longest] + 1) % array.shape[longest]] + index_at[longest + 1:]
    return array.at[tuple(index_at)].set(smallest).at[tuple(next_to)].set(high)


def level_of(own_key, extent, pieces, smallest, largest):
    level, own = 1.0, jax.random.fold_in(own_key, 6)
    for dim, blocks in pieces:
        steps = jnp.exp(jax.random.uniform(jax.random.fold_in(own, dim), (blocks,), jnp.float32, smallest / len(pieces), largest / len(pieces)))
        level = level * jnp.repeat(steps, extent[dim] // blocks).reshape([-1 if axis == dim else 1 for axis in range(len(extent))])
    return level


def shared_out(stream_key, own, number, rows, number_of, top, most, lean):
    order = jax.random.permutation(stream_key, number_of)
    heavy_load, usual = load_shares(number_of, rows * top, most, lean, True), load_shares(number_of, rows * top, most, lean, False)
    places = jnp.arange(number_of)

    def named(lengths, turn):
        used = int((lengths > 0).sum())
        fixed = max(1, used // 4)
        moved = fixed + (places - fixed + turn * (used - fixed)) % max(1, number_of - fixed)
        return jnp.zeros((number_of,), jnp.int32).at[order[jnp.where(places < fixed, places, moved)]].set(jnp.asarray(lengths, jnp.int32))

    lengths = jnp.where(number % 4 == 0, named(heavy_load, number // 4), named(usual, number - number // 4 - 1))
    mixed = jax.random.permutation(jax.random.fold_in(own, 3), number_of)
    donor, taker = mixed[0:number_of // 2 * 2:2], mixed[1:number_of // 2 * 2:2]
    slack = jnp.minimum(lengths[donor] - 1, most - lengths[taker]) // 2
    slack = jnp.where((donor == order[0]) | (taker == order[0]) | (lengths[taker] == 0), 0, jnp.maximum(slack, 0))
    moved = jax.random.randint(jax.random.fold_in(own, 4), (number_of // 2,), 0, 1 << 20) % (slack + 1)
    lengths = lengths.at[donor].add(-moved).at[taker].add(moved)
    labels = jnp.searchsorted(jnp.cumsum(lengths), jnp.arange(rows * top), side="right").astype(jnp.int32)
    table = labels.reshape(top, rows).T
    table = table[jax.random.permutation(jax.random.fold_in(own, 1), rows)]
    turn = jax.random.randint(jax.random.fold_in(own, 2), (rows, 1), 0, top)
    return jnp.take_along_axis(table, (jnp.arange(top)[None, :] + turn) % top, axis=1)


def load_shares(amount, total, reach, skew, full):
    loads = [(1 << 20) // math.isqrt(grade ** skew) + 1 for grade in range(1, amount + 1)]
    largest = reach if full else min(reach, max(-(-total // amount), total * loads[0] // sum(loads)))
    least = 1 if total - largest >= amount - 1 else 0
    holding, spare = [largest] + [least] * (amount - 1), total - largest - least * (amount - 1)
    while spare > 0:
        candidates = [i for i in range(1, amount) if holding[i] < largest] or [i for i in range(1, amount) if holding[i] < reach]
        pool, remaining = sum([loads[i] for i in candidates]), spare
        for i in candidates:
            extra = min(reach - holding[i], max(1, remaining * loads[i] // pool), spare)
            holding[i] = holding[i] + extra
            spare = spare - extra
    return np.array(holding)


def setup_inputs(seed: int = 0) -> dict:
    splits = jax.random.split(jax.random.key(seed), 5)
    swath_intensities = jnp.clip(jnp.exp(math.log(1.0) - 4.61031033 * jax.random.uniform(splits[0], (PASSES_ALTOGETHER, SWATHS_ALTOGETHER, SWATH_HEIGHT, 2, RASTER_BREADTH), jnp.float32) ** level_of(splits[0], (PASSES_ALTOGETHER, SWATHS_ALTOGETHER, SWATH_HEIGHT, 2, RASTER_BREADTH), ((0, 4), (1, 8)), -0.2, 0.2)), 0.0099487305, 1.0).astype(jnp.bfloat16)
    destination_patch_keys = jax.random.split(jax.random.fold_in(splits[1], 1), SWATHS_ALTOGETHER // SWATHS_HELD)
    destination_patch_turns = jax.random.permutation(jax.random.fold_in(splits[1], 3), SWATHS_ALTOGETHER // SWATHS_HELD)
    destination_patch = jax.vmap(lambda own, number: shared_out(jax.random.fold_in(splits[1], 2), own, number, SWATHS_HELD, N_TILE, 1, SHIPMENT_BOUND, 1))(destination_patch_keys, destination_patch_turns).reshape((SWATHS_ALTOGETHER, 1))
    swath_leading_scanline = touch_ends(jax.random.randint(splits[2], (SWATHS_ALTOGETHER,), 0, PATCH_HEIGHT - SWATH_HEIGHT + 1), jax.random.fold_in(splits[2], 1), 0, PATCH_HEIGHT - SWATH_HEIGHT).astype(jnp.int32)
    receiver_floor_intensity = jnp.clip(jnp.exp(math.log(1.0) - 2.3025851 * jax.random.uniform(splits[3], (PASSES_ALTOGETHER, N_TILE * PATCH_HEIGHT, 2, RASTER_BREADTH), jnp.float32) ** level_of(splits[3], (PASSES_ALTOGETHER, N_TILE * PATCH_HEIGHT, 2, RASTER_BREADTH), ((0, 4), (1, 8)), -0.2, 0.2)), 0.1, 1.0)
    return dict(swath_intensities=swath_intensities, destination_patch=destination_patch, swath_leading_scanline=swath_leading_scanline, receiver_floor_intensity=receiver_floor_intensity)


def box_mean(field, row_axis, col_axis):
    total = field
    scale = jnp.ones((), jnp.float32)
    for axis in (row_axis, col_axis):
        length = field.shape[axis]
        widths = [(0, 0)] * field.ndim
        widths[axis] = (3, 3)
        padded = jnp.pad(total, widths)
        summed = lax.slice_in_dim(padded, 0, length, axis=axis)
        for shift_by in range(1, 7):
            summed = summed + lax.slice_in_dim(padded, shift_by, shift_by + length, axis=axis)
        total = summed
        places = jnp.arange(length, dtype=jnp.int32)
        counted = (jnp.minimum(places + 3, length - 1) - jnp.maximum(places - 3, 0) + 1).astype(jnp.float32)
        view = [1] * field.ndim
        view[axis] = length
        scale = scale * counted.reshape(view)
    return total / scale


def reference(swath_intensities, destination_patch, swath_leading_scanline, receiver_floor_intensity):
    first_rows = (destination_patch[:, 0] * PATCH_HEIGHT + swath_leading_scanline).astype(jnp.int32)

    def insert_swath(swath_ordinal, raster_patch):
        leading_scanline = first_rows[swath_ordinal]
        single_swath = swath_intensities[:, swath_ordinal].astype(jnp.float32)
        running_patch = lax.dynamic_slice_in_dim(raster_patch, leading_scanline, SWATH_HEIGHT, 1)
        return lax.dynamic_update_slice_in_dim(raster_patch, running_patch + single_swath, leading_scanline, 1)

    raster_patch = lax.fori_loop(0, SWATHS_ALTOGETHER, insert_swath, receiver_floor_intensity.astype(jnp.float32))
    tiles = raster_patch.reshape(PASSES_ALTOGETHER, N_TILE, PATCH_HEIGHT, 2, RASTER_BREADTH)
    means = box_mean(tiles, 2, 4)
    ratio_sum = jnp.sum(tiles / means, axis=0) / PASSES_ALTOGETHER
    filtered = (means * ratio_sum).astype(jnp.bfloat16)
    return filtered.reshape(PASSES_ALTOGETHER, N_TILE * PATCH_HEIGHT, 2, RASTER_BREADTH)
```

```python
import functools

import jax
import jax.numpy as jnp
from jax import lax
from jax.experimental import pallas as pl
from jax.experimental.pallas import tpu as pltpu
from jax.sharding import PartitionSpec as P

LANES = 128
REACH = 3
LIMIT = {"place": 16, "merge": 12, "box": 8, "add": 4, "scale": 4}
VMEM = pl.BlockSpec(memory_space=pltpu.VMEM)
SMEM = pl.BlockSpec(memory_space=pltpu.SMEM)


def pack(array):
    *lead, pols, cols = array.shape
    axis = len(lead)
    array = array.reshape(*lead, pols, cols // LANES, LANES)
    return jnp.swapaxes(array, axis, axis + 1).reshape(*lead, pols * cols // LANES, LANES)


def unpack(array, pols):
    *lead, subs, _ = array.shape
    axis = len(lead)
    array = array.reshape(*lead, subs // pols, pols, LANES)
    return jnp.swapaxes(array, axis, axis + 1).reshape(*lead, pols, subs // pols * LANES)


def place_kernel(chips, owner_ref, lead_ref, swath_ref, other_ref, own_ref, acc):
    blocks, scan, _, _ = swath_ref.shape
    rows = own_ref.shape[1]
    me = lax.axis_index("tile")
    core, chip = me % 2, me // 2
    step = 8

    def clear(i, carry):
        acc[pl.ds(i * step, step)] = jnp.zeros((step,) + acc.shape[1:], acc.dtype)
        return carry

    lax.fori_loop(0, acc.shape[0] // step, clear, 0, unroll=2)

    def insert(block, carry):
        owner = owner_ref[block]
        slot = lax.rem(owner // 2 - chip + chips, chips)
        slot = jnp.where(owner % 2 == core, slot + chips, slot)
        base = slot * rows + lead_ref[block]

        def part(i, c):
            span = pl.ds(base + i * step, step)
            acc[span] = acc[span] + swath_ref[block, pl.ds(i * step, step)].astype(jnp.float32)
            return c

        return lax.fori_loop(0, scan // step, part, carry, unroll=True)

    lax.fori_loop(0, blocks, insert, 0)

    def emit(i, carry):
        for slot in range(chips):
            span = pl.ds(i * step, step)
            other_ref[slot, span] = acc[pl.ds(slot * rows + i * step, step)].astype(other_ref.dtype)
            own_ref[slot, span] = acc[pl.ds((chips + slot) * rows + i * step, step)]
        return carry

    lax.fori_loop(0, rows // step, emit, 0)


def merge_kernel(own_ref, came_ref, keep_ref, *send_refs):
    rows = keep_ref.shape[0]
    step = 8

    def part(i, carry):
        span = pl.ds(i * step, step)
        keep_ref[span] = own_ref[0, span] + came_ref[0, span].astype(jnp.float32)
        for slot, send in enumerate(send_refs, 1):
            send[span] = (own_ref[slot, span] + came_ref[slot, span].astype(jnp.float32)).astype(send.dtype)
        return carry

    lax.fori_loop(0, rows // step, part, 0)


def box_kernel(pols, *refs):
    keep_ref, floor_ref, *came_refs, means_ref, ratio_ref, first_ref, second_ref, canvas, down = refs
    rows, subs, _ = keep_ref.shape
    half = rows // 2
    step = 8
    zero = jnp.zeros((step, subs, LANES), jnp.float32)
    canvas[pl.ds(0, step)] = zero
    canvas[pl.ds(rows + step, step)] = zero

    def gather(i, carry):
        span = pl.ds(i * step, step)
        total = keep_ref[span] + floor_ref[span]
        for came in came_refs:
            total = total + came[span].astype(jnp.float32)
        canvas[pl.ds(i * step + step, step)] = total
        return carry

    lax.fori_loop(0, rows // step, gather, 0)

    sub = lax.broadcasted_iota(jnp.int32, (step, subs, LANES), 1)
    lane = lax.broadcasted_iota(jnp.int32, (step, subs, LANES), 2)
    row = lax.broadcasted_iota(jnp.int32, (step, subs, LANES), 0)
    col = sub // pols * LANES + lane
    cols = subs // pols * LANES
    counted_cols = jnp.minimum(col + REACH, cols - 1) - jnp.maximum(col - REACH, 0) + 1

    def ahead(x, by):
        after = jnp.where(sub < subs - pols, pltpu.roll(x, subs - pols, 1), 0.0)
        return pltpu.roll(jnp.where(lane < by, after, x), LANES - by, 2)

    def behind(x, by):
        before = jnp.where(sub >= pols, pltpu.roll(x, pols, 1), 0.0)
        return pltpu.roll(jnp.where(lane >= LANES - by, before, x), by, 2)

    def box(i, carry):
        at = i * step + step
        centre = canvas[pl.ds(at, step)]
        total = centre
        for shift in range(-REACH, REACH + 1):
            if shift:
                total = total + canvas[pl.ds(at + shift, step)]
        triple = behind(total, 1) + total + ahead(total, 1)
        total = behind(triple, 2) + total + ahead(triple, 2)
        place = row + i * step
        counted_rows = jnp.minimum(place + REACH, rows - 1) - jnp.maximum(place - REACH, 0) + 1
        means = total / (counted_rows * counted_cols).astype(jnp.float32)
        ratio = centre / means
        span = pl.ds(i * step, step)
        means_ref[span] = means
        ratio_ref[span] = ratio
        return ratio

    def upper(i, carry):
        first_ref[pl.ds(i * step, step)] = box(i, 0).astype(first_ref.dtype)
        return carry

    def lower(i, carry):
        second_ref[pl.ds(i * step, step)] = box(i + half // step, 0).astype(second_ref.dtype)
        return carry

    lax.fori_loop(0, half // step, upper, 0)
    lax.fori_loop(0, half // step, lower, 0)


def add_kernel(ratio_ref, first_ref, second_ref, sum_ref, next_first_ref, next_second_ref):
    half = first_ref.shape[0]
    step = 8

    def part(i, carry):
        span, lower = pl.ds(i * step, step), pl.ds(half + i * step, step)
        upper_sum = ratio_ref[span] + first_ref[span].astype(jnp.float32)
        lower_sum = ratio_ref[lower] + second_ref[span].astype(jnp.float32)
        sum_ref[span], sum_ref[lower] = upper_sum, lower_sum
        next_first_ref[span] = upper_sum.astype(next_first_ref.dtype)
        next_second_ref[span] = lower_sum.astype(next_second_ref.dtype)
        return carry

    lax.fori_loop(0, half // step, part, 0)


def scale_kernel(dates, means_ref, sum_ref, first_ref, second_ref, out_ref):
    half = first_ref.shape[0]
    step = 8

    def part(i, carry):
        for start, came in ((0, first_ref), (half, second_ref)):
            span = pl.ds(start + i * step, step)
            total = (sum_ref[span] + came[pl.ds(i * step, step)].astype(jnp.float32)) / dates
            out_ref[span] = (means_ref[span] * total).astype(out_ref.dtype)
        return carry

    lax.fori_loop(0, half // step, part, 0)


def per_device(tiles, dates, swaths, patch, lead, floor):
    chips = tiles // 2
    pols = swaths.shape[3]
    swaths, floor = pack(swaths[0]), pack(floor[0])
    rows, subs, _ = floor.shape
    full = (rows, subs, LANES)
    part = (rows // 2, subs, LANES)
    f32, bf16 = jnp.float32, jnp.bfloat16
    struct = jax.ShapeDtypeStruct

    other, own = pl.pallas_call(
        functools.partial(place_kernel, chips),
        out_shape=(struct((chips,) + full, bf16), struct((chips,) + full, f32)),
        in_specs=[SMEM, SMEM, VMEM],
        out_specs=(VMEM, VMEM),
        scratch_shapes=[pltpu.VMEM((2 * chips * rows, subs, LANES), f32)],
        name="place",
        compiler_params=pltpu.CompilerParams(vmem_limit_bytes=LIMIT["place"] << 20),
    )(patch[:, 0], lead, swaths)

    came = lax.ppermute(other, "tile", [(t, t ^ 1) for t in range(tiles)])

    keep, *sends = pl.pallas_call(
        merge_kernel,
        out_shape=(struct(full, f32),) + (struct(full, bf16),) * (chips - 1),
        in_specs=[VMEM, VMEM],
        out_specs=(VMEM,) * chips,
        name="merge",
        compiler_params=pltpu.CompilerParams(vmem_limit_bytes=LIMIT["merge"] << 20),
    )(own, came)

    arrived = []
    for shift, send in enumerate(sends, 1):
        pairs = [(t, (t + 2 * shift) % tiles) for t in range(tiles)]
        arrived.append(lax.ppermute(send, "tile", pairs))

    means, ratio, first, second = pl.pallas_call(
        functools.partial(box_kernel, pols),
        out_shape=(struct(full, f32), struct(full, f32), struct(part, bf16), struct(part, bf16)),
        in_specs=[VMEM] * (chips + 1),
        out_specs=(VMEM,) * 4,
        scratch_shapes=[pltpu.VMEM((rows + 16, subs, LANES), f32), pltpu.VMEM((8, subs, LANES), f32)],
        name="box",
        compiler_params=pltpu.CompilerParams(vmem_limit_bytes=LIMIT["box"] << 20),
    )(keep, floor, *arrived)

    one = [(d, d ^ 1) for d in range(dates)]
    two = [(d, d ^ 2) for d in range(dates)]
    first = lax.ppermute(first, "date", one)
    second = lax.ppermute(second, "date", two)
    total, first, second = pl.pallas_call(
        add_kernel,
        out_shape=(struct(full, f32), struct(part, bf16), struct(part, bf16)),
        in_specs=[VMEM] * 3,
        out_specs=(VMEM,) * 3,
        name="add",
        compiler_params=pltpu.CompilerParams(vmem_limit_bytes=LIMIT["add"] << 20),
    )(ratio, first, second)
    first = lax.ppermute(first, "date", two)
    second = lax.ppermute(second, "date", one)
    out = pl.pallas_call(
        functools.partial(scale_kernel, float(dates)),
        out_shape=struct(full, bf16),
        in_specs=[VMEM] * 4,
        out_specs=VMEM,
        name="scale",
        compiler_params=pltpu.CompilerParams(vmem_limit_bytes=LIMIT["scale"] << 20),
    )(means, total, first, second)
    return unpack(out, pols)[None]


def solution(mesh):
    return jax.shard_map(
        functools.partial(per_device, mesh.shape["tile"], mesh.shape["date"]),
        mesh=mesh,
        in_specs=(
            P("date", "tile", None, None, None),
            P("tile", None),
            P("tile"),
            P("date", "tile", None, None),
        ),
        out_specs=P("date", "tile", None, None),
        check_vma=False,
    )
```

```python
import functools

import jax
import jax.numpy as jnp
from jax import lax
from jax.experimental import pallas as pl
from jax.experimental.pallas import tpu as pltpu
from jax.sharding import PartitionSpec as P

LANES = 128
REACH = 3
STEP = 8
VMEM = pl.BlockSpec(memory_space=pltpu.VMEM)
HBM = pl.BlockSpec(memory_space=pltpu.HBM)
F32, BF16 = jnp.float32, jnp.bfloat16


def pack(array):
    *lead, pols, cols = array.shape
    axis = len(lead)
    array = array.reshape(*lead, pols, cols // LANES, LANES)
    return jnp.swapaxes(array, axis, axis + 1).reshape(*lead, pols * cols // LANES, LANES)


def unpack(array, pols):
    *lead, subs, _ = array.shape
    axis = len(lead)
    array = array.reshape(*lead, subs // pols, pols, LANES)
    return jnp.swapaxes(array, axis, axis + 1).reshape(*lead, pols, subs // pols * LANES)


def rows_loop(count, body, unroll=1):
    lax.fori_loop(0, count // STEP, lambda i, c: (body(pl.multiple_of(i * STEP, STEP)), c)[1], 0, unroll=unroll)


def slot_of(relay, chips, owner_chip, chip):
    return owner_chip ^ chip if relay else lax.rem(owner_chip - chip + chips, chips)


def place_kernel(relay, chips, early, owner_hbm, lead_hbm, swath_hbm, *refs):
    early_ref, other_ref, own_ref, acc, swath, owner, lead, sems = refs
    blocks, scan, _, _ = swath.shape
    rows = own_ref.shape[1]
    me = lax.axis_index("tile")
    core, chip = me % 2, me // 2
    small = (
        pltpu.make_async_copy(owner_hbm, owner, sems.at[blocks]),
        pltpu.make_async_copy(lead_hbm, lead, sems.at[blocks + 1]),
    )
    for copy in small:
        copy.start()

    def fetch(block):
        return pltpu.make_async_copy(swath_hbm.at[block], swath.at[block], sems.at[block])

    for block in range(blocks):
        fetch(block).start()

    def clear(at):
        zero = jnp.zeros((STEP,) + acc.shape[2:], F32)
        for slot in range(chips):
            acc[slot, pl.ds(at, STEP)] = zero
            own_ref[slot, pl.ds(at, STEP)] = zero

    rows_loop(rows, clear)
    for copy in small:
        copy.wait()

    def add_into(ref, slot, block, base):
        for row in range(0, scan, STEP):
            span = pl.ds(base + row, STEP)
            ref[slot, span] = ref[slot, span] + swath[block, pl.ds(row, STEP)].astype(F32)

    def insert(block, carry):
        target = owner[block]
        base = lead[block]
        slot = slot_of(relay, chips, target // 2, chip)
        fetch(block).wait()

        @pl.when(target % 2 == core)
        def _():
            add_into(own_ref, slot, block, base)

        @pl.when(target % 2 != core)
        def _():
            add_into(acc, slot, block, base)

        return carry

    lax.fori_loop(0, blocks, insert, 0)
    others = [slot for slot in range(chips) if slot != early]

    def emit(at):
        span = pl.ds(at, STEP)
        early_ref[span] = acc[early, span].astype(BF16)
        for place, slot in enumerate(others):
            other_ref[place, span] = acc[slot, span].astype(BF16)

    rows_loop(rows, emit)


def merge_early_kernel(early, own_ref, came_ref, send_ref):
    def part(at):
        span = pl.ds(at, STEP)
        send_ref[span] = (own_ref[early, span] + came_ref[span].astype(F32)).astype(BF16)

    rows_loop(send_ref.shape[0], part)


def merge_kernel(slots, own_ref, floor_ref, came_ref, keep_ref, *send_refs):
    def part(at):
        span = pl.ds(at, STEP)
        for place, slot in enumerate(slots):
            total = own_ref[slot, span] + came_ref[place, span].astype(F32)
            if place:
                send_refs[place - 1][span] = total.astype(BF16)
            else:
                keep_ref[span] = total + floor_ref[span]

    rows_loop(keep_ref.shape[0], part)


def relay_kernel(far_ref, passing_ref, send_ref):
    def part(at):
        span = pl.ds(at, STEP)
        send_ref[span] = (far_ref[span].astype(F32) + passing_ref[span].astype(F32)).astype(BF16)

    rows_loop(send_ref.shape[0], part)


def box_kernel(relay, pols, keep_ref, *refs):
    *came_refs, means_ref, ratio_ref, send_ref, canvas = refs
    rows, subs, _ = keep_ref.shape
    zero = jnp.zeros((STEP, subs, LANES), F32)
    canvas[pl.ds(0, STEP)] = zero
    canvas[pl.ds(rows + STEP, STEP)] = zero

    def gather(refs):
        def part(at):
            span = pl.ds(at, STEP)
            total = keep_ref[span]
            for came in refs:
                total = total + came[span].astype(F32)
            canvas[pl.ds(at + STEP, STEP)] = total

        rows_loop(rows, part)

    if relay:
        first, direct, passed, near = came_refs
        chip = lax.axis_index("tile") // 2
        ends = (chip == 0) | (chip == 3)
        pl.when(ends)(lambda: gather((first, direct, near)))
        pl.when(jnp.logical_not(ends))(lambda: gather((passed, near)))
    else:
        gather(came_refs)

    shape = (STEP, subs, LANES)
    sub = lax.broadcasted_iota(jnp.int32, shape, 1)
    lane = lax.broadcasted_iota(jnp.int32, shape, 2)
    cols = subs // pols * LANES

    def counted(place, length):
        return jnp.minimum(place + REACH, length - 1) - jnp.maximum(place - REACH, 0) + 1

    col_scale = 1.0 / counted(sub // pols * LANES + lane, cols).astype(F32)

    def ahead(x, by):
        after = jnp.where(sub < subs - pols, pltpu.roll(x, subs - pols, 1), 0.0)
        return pltpu.roll(jnp.where(lane < by, after, x), LANES - by, 2)

    def behind(x, by):
        before = jnp.where(sub >= pols, pltpu.roll(x, pols, 1), 0.0)
        return pltpu.roll(jnp.where(lane >= LANES - by, before, x), by, 2)

    def box(at, scale):
        x = canvas[pl.ds(at + STEP - REACH, STEP + 2 * REACH)]
        two = x[:-1] + x[1:]
        four = two[:-2] + two[2:]
        total = four[:STEP] + two[4 : 4 + STEP] + x[6 : 6 + STEP]
        triple = behind(total, 1) + total + ahead(total, 1)
        total = behind(triple, 2) + total + ahead(triple, 2)
        means = total * scale
        ratio = x[REACH : REACH + STEP] / means
        span = pl.ds(at, STEP)
        means_ref[span] = means
        ratio_ref[span] = ratio
        send_ref[span] = ratio.astype(BF16)

    row = lax.broadcasted_iota(jnp.int32, shape, 0)
    for at in (0, rows - STEP):
        box(at, col_scale / counted(row + at, rows).astype(F32))
    inner = col_scale * (1.0 / (2 * REACH + 1))
    lax.fori_loop(1, rows // STEP - 1, lambda i, c: (box(pl.multiple_of(i * STEP, STEP), inner), c)[1], 0)


def add_kernel(ratio_ref, came_ref, sum_ref, send_ref):
    def part(at):
        span = pl.ds(at, STEP)
        total = ratio_ref[span] + came_ref[span].astype(F32)
        sum_ref[span] = total
        send_ref[span] = total.astype(BF16)

    rows_loop(sum_ref.shape[0], part)


def scale_kernel(dates, means_ref, sum_ref, came_ref, out_ref):
    def part(at):
        span = pl.ds(at, STEP)
        total = (sum_ref[span] + came_ref[span].astype(F32)) / dates
        out_ref[span] = (means_ref[span] * total).astype(BF16)

    rows_loop(out_ref.shape[0], part)


def call(kernel, name, outs, ins, specs=None, mib=8, scratch=()):
    return pl.pallas_call(
        kernel,
        out_shape=outs,
        in_specs=specs or [VMEM] * len(ins),
        out_specs=jax.tree.map(lambda _: VMEM, outs),
        scratch_shapes=scratch,
        name=name,
        compiler_params=pltpu.CompilerParams(vmem_limit_bytes=mib << 20),
    )(*ins)


def per_device(tiles, dates, swaths, patch, lead, floor):
    chips = tiles // 2
    relay = chips == 4
    pols = swaths.shape[3]
    swaths, floor = pack(swaths[0]), pack(floor[0])
    blocks = swaths.shape[0]
    rows, subs, _ = floor.shape
    full = (rows, subs, LANES)
    wide = jax.ShapeDtypeStruct(full, F32)
    thin = jax.ShapeDtypeStruct(full, BF16)

    early = 2 if relay else 1
    slots = [0, 3, 1] if relay else [s for s in range(chips) if s != early]
    canvases = 4 * rows * subs * LANES * chips
    early_out, other, own = call(
        functools.partial(place_kernel, relay, chips, early),
        "place",
        (thin, jax.ShapeDtypeStruct((chips - 1,) + full, BF16), jax.ShapeDtypeStruct((chips,) + full, F32)),
        tuple(pltpu.with_memory_space_constraint(a, pltpu.HBM) for a in (patch[:, 0], lead, swaths)),
        specs=[HBM] * 3,
        mib=(3 * canvases >> 20) + 4,
        scratch=[
            pltpu.VMEM((chips,) + full, F32),
            pltpu.VMEM(swaths.shape, BF16),
            pltpu.SMEM((blocks,), jnp.int32),
            pltpu.SMEM((blocks,), jnp.int32),
            pltpu.SemaphoreType.DMA((blocks + 2,)),
        ],
    )
    partner = [(t, t ^ 1) for t in range(tiles)]
    early_came = lax.ppermute(early_out, "tile", partner)
    came = lax.ppermute(other, "tile", partner)
    early_send = call(functools.partial(merge_early_kernel, early), "merge_early", thin, (own, early_came))

    def along(array, moves):
        return lax.ppermute(array, "tile", [(2 * a + core, 2 * b + core) for a, b in moves for core in range(2)])

    ordered = [s for s in range(chips) if s != early]
    if relay:
        first = along(early_send, [(0, 1), (3, 2), (1, 3), (2, 0)])
    else:
        first = along(early_send, [(c, (c + early) % chips) for c in range(chips)])
    keep, *sends = call(
        functools.partial(merge_kernel, ordered),
        "merge",
        (wide,) + (thin,) * (chips - 2),
        (own, floor, came),
        mib=(2 * canvases >> 20) + 4,
    )
    if relay:
        near_send, far_send = sends
        direct = along(far_send, [(0, 3), (3, 0), (1, 1), (2, 2)])
        near = along(near_send, [(0, 1), (1, 0), (2, 3), (3, 2)])
        passing = call(relay_kernel, "relay", thin, (far_send, first))
        passed = along(passing, [(1, 2), (2, 1), (0, 0), (3, 3)])
        arrived = [first, direct, passed, near]
    else:
        arrived = [first]
        for shift, send in zip(ordered[1:], sends):
            arrived.append(along(send, [(c, (c + shift) % chips) for c in range(chips)]))

    means, total, send = call(
        functools.partial(box_kernel, relay, pols),
        "box",
        (wide, wide, thin),
        (keep, *arrived),
        mib=8 if relay else 16,
        scratch=[pltpu.VMEM((rows + 2 * STEP, subs, LANES), F32)],
    )

    bits = [1 << b for b in range(dates.bit_length() - 1)]
    for step, (even, odd) in enumerate(zip(bits, bits[::-1]), 1):
        pairs = [
            (d * tiles + t, (d ^ (odd if t % 2 else even)) * tiles + t) for d in range(dates) for t in range(tiles)
        ]
        came = lax.ppermute(send, ("date", "tile"), pairs)
        if step < len(bits):
            total, send = call(add_kernel, "add", (wide, thin), (total, came), mib=4)
    out = call(functools.partial(scale_kernel, float(dates)), "scale", thin, (means, total, came), mib=4)
    return unpack(out, pols)[None]


def solution(mesh):
    return jax.shard_map(
        functools.partial(per_device, mesh.shape["tile"], mesh.shape["date"]),
        mesh=mesh,
        in_specs=(
            P("date", "tile", None, None, None),
            P("tile", None),
            P("tile"),
            P("date", "tile", None, None),
        ),
        out_specs=P("date", "tile", None, None),
        check_vma=False,
    )
```

```python
import functools

import jax
import jax.numpy as jnp
from jax import lax
from jax.experimental import pallas as pl
from jax.experimental.pallas import tpu as pltpu
from jax.sharding import PartitionSpec as P


LANES = 128
REACH = 3
STEP = 8
VMEM = pl.BlockSpec(memory_space=pltpu.VMEM)
HBM = pl.BlockSpec(memory_space=pltpu.HBM)
F32, BF16 = jnp.float32, jnp.bfloat16


def pack(array):
    *lead, pols, cols = array.shape
    axis = len(lead)
    array = array.reshape(*lead, pols, cols // LANES, LANES)
    return jnp.swapaxes(array, axis, axis + 1).reshape(*lead, pols * cols // LANES, LANES)


def unpack(array, pols):
    *lead, subs, _ = array.shape
    axis = len(lead)
    array = array.reshape(*lead, subs // pols, pols, LANES)
    return jnp.swapaxes(array, axis, axis + 1).reshape(*lead, pols, subs // pols * LANES)


def rows_loop(count, body, unroll=1):
    lax.fori_loop(0, count // STEP, lambda i, c: (body(pl.multiple_of(i * STEP, STEP)), c)[1], 0, unroll=unroll)


def slot_of(relay, chips, owner_chip, chip):
    return owner_chip ^ chip if relay else lax.rem(owner_chip - chip + chips, chips)


def place_kernel(relay, chips, early, owner_hbm, lead_hbm, swath_hbm, *refs):
    early_ref, other_ref, own_ref, acc, swath, owner, lead, sems = refs
    blocks, scan, _, _ = swath.shape
    rows = own_ref.shape[1]
    me = lax.axis_index("tile")
    core, chip = me % 2, me // 2
    small = (
        pltpu.make_async_copy(owner_hbm, owner, sems.at[blocks]),
        pltpu.make_async_copy(lead_hbm, lead, sems.at[blocks + 1]),
    )
    for copy in small:
        copy.start()

    def fetch(block):
        return pltpu.make_async_copy(swath_hbm.at[block], swath.at[block], sems.at[block])

    for block in range(blocks):
        fetch(block).start()

    def clear(at):
        zero = jnp.zeros((STEP,) + acc.shape[2:], F32)
        for slot in range(chips):
            acc[slot, pl.ds(at, STEP)] = zero
            own_ref[slot, pl.ds(at, STEP)] = zero

    rows_loop(rows, clear)
    for copy in small:
        copy.wait()

    def add_into(ref, slot, block, base):
        for row in range(0, scan, STEP):
            span = pl.ds(base + row, STEP)
            ref[slot, span] = ref[slot, span] + swath[block, pl.ds(row, STEP)].astype(F32)

    def insert(block, carry):
        target = owner[block]
        base = lead[block]
        slot = slot_of(relay, chips, target // 2, chip)
        fetch(block).wait()

        @pl.when(target % 2 == core)
        def _():
            add_into(own_ref, slot, block, base)

        @pl.when(target % 2 != core)
        def _():
            add_into(acc, slot, block, base)

        return carry

    lax.fori_loop(0, blocks, insert, 0)
    others = [slot for slot in range(chips) if slot != early]

    def emit(at):
        span = pl.ds(at, STEP)
        early_ref[span] = acc[early, span].astype(BF16)
        for place, slot in enumerate(others):
            other_ref[place, span] = acc[slot, span].astype(BF16)

    rows_loop(rows, emit)


def merge_early_kernel(early, own_ref, came_ref, send_ref):
    def part(at):
        span = pl.ds(at, STEP)
        send_ref[span] = (own_ref[early, span] + came_ref[span].astype(F32)).astype(BF16)

    rows_loop(send_ref.shape[0], part)


def merge_kernel(slots, own_ref, floor_ref, came_ref, keep_ref, *send_refs):
    def part(at):
        span = pl.ds(at, STEP)
        for place, slot in enumerate(slots):
            total = own_ref[slot, span] + came_ref[place, span].astype(F32)
            if place:
                send_refs[place - 1][span] = total.astype(BF16)
            else:
                keep_ref[span] = total + floor_ref[span]

    rows_loop(keep_ref.shape[0], part)


def relay_kernel(far_ref, passing_ref, send_ref):
    def part(at):
        span = pl.ds(at, STEP)
        send_ref[span] = (far_ref[span].astype(F32) + passing_ref[span].astype(F32)).astype(BF16)

    rows_loop(send_ref.shape[0], part)


def box_kernel(relay, pols, keep_ref, *refs):
    *came_refs, means_ref, ratio_ref, upper_ref, lower_ref, canvas = refs
    rows, subs, _ = keep_ref.shape
    zero = jnp.zeros((STEP, subs, LANES), F32)
    canvas[pl.ds(0, STEP)] = zero
    canvas[pl.ds(rows + STEP, STEP)] = zero

    def gather(refs):
        def part(at):
            span = pl.ds(at, STEP)
            total = keep_ref[span]
            for came in refs:
                total = total + came[span].astype(F32)
            canvas[pl.ds(at + STEP, STEP)] = total

        rows_loop(rows, part)

    if relay:
        first, direct, passed, near = came_refs
        chip = lax.axis_index("tile") // 2
        ends = (chip == 0) | (chip == 3)
        pl.when(ends)(lambda: gather((first, direct, near)))
        pl.when(jnp.logical_not(ends))(lambda: gather((passed, near)))
    else:
        gather(came_refs)

    shape = (STEP, subs, LANES)
    sub = lax.broadcasted_iota(jnp.int32, shape, 1)
    lane = lax.broadcasted_iota(jnp.int32, shape, 2)
    cols = subs // pols * LANES

    def counted(place, length):
        return jnp.minimum(place + REACH, length - 1) - jnp.maximum(place - REACH, 0) + 1

    col_scale = 1.0 / counted(sub // pols * LANES + lane, cols).astype(F32)

    def ahead(x, by):
        after = jnp.where(sub < subs - pols, pltpu.roll(x, subs - pols, 1), 0.0)
        return pltpu.roll(jnp.where(lane < by, after, x), LANES - by, 2)

    def behind(x, by):
        before = jnp.where(sub >= pols, pltpu.roll(x, pols, 1), 0.0)
        return pltpu.roll(jnp.where(lane >= LANES - by, before, x), by, 2)

    edge_ahead = (sub >= subs - pols) & (lane == LANES - 2)
    edge_behind = (sub < pols) & (lane == 1)

    def box(at, scale, send_ref):
        x = canvas[pl.ds(at + STEP - REACH, STEP + 2 * REACH)]
        two = x[:-1] + x[1:]
        four = two[:-2] + two[2:]
        total = four[:STEP] + two[4 : 4 + STEP] + x[6 : 6 + STEP]
        right, left = ahead(total, 1), behind(total, 1)
        triple = left + total + right
        edge = jnp.where(edge_ahead, right, jnp.where(edge_behind, left, 0.0))
        total = behind(triple, 2) + (total + edge) + ahead(triple, 2)
        means = total * scale
        ratio = x[REACH : REACH + STEP] / means
        span = pl.ds(at, STEP)
        means_ref[span] = means
        ratio_ref[span] = ratio
        send_ref[pl.ds(at % (rows // 2), STEP)] = ratio.astype(BF16)

    row = lax.broadcasted_iota(jnp.int32, shape, 0)
    inner = col_scale * (1.0 / (2 * REACH + 1))
    for at in range(0, rows, STEP):
        outer = at in (0, rows - STEP)
        scale = col_scale / counted(row + at, rows).astype(F32) if outer else inner
        box(at, scale, (upper_ref, lower_ref)[2 * at // rows])


def add_kernel(start, ratio_ref, came_ref, sum_ref, send_ref):
    def part(at):
        span = pl.ds(at, STEP)
        total = ratio_ref[pl.ds(at + start, STEP)] + came_ref[span].astype(F32)
        sum_ref[span] = total
        send_ref[span] = total.astype(BF16)

    rows_loop(sum_ref.shape[0], part, unroll=True)


def scale_kernel(dates, start, means_ref, sum_ref, came_ref, *refs):
    out_hbm, out, sems = refs[-3:]
    rows = sum_ref.shape[0]
    pieces = 2
    size = rows // pieces

    def copy(piece):
        here = pl.ds(piece * size, size)
        return pltpu.make_async_copy(out.at[here], out_hbm.at[pl.ds(start + piece * size, size)], sems.at[piece])

    for piece in range(pieces):
        for at in range(piece * size, piece * size + size, STEP):
            span = pl.ds(at, STEP)
            total = (sum_ref[span] + came_ref[span].astype(F32)) * (1.0 / dates)
            out[span] = (means_ref[pl.ds(start + at, STEP)] * total).astype(BF16)
        copy(piece).start()
    for piece in range(pieces):
        copy(piece).wait()


def call(kernel, outs, ins, specs=None, mib=8, scratch=(), out_specs=None, aliases=None):
    return pl.pallas_call(
        kernel,
        out_shape=outs,
        in_specs=specs or [VMEM] * len(ins),
        out_specs=out_specs or jax.tree.map(lambda _: VMEM, outs),
        scratch_shapes=scratch,
        input_output_aliases=aliases or {},
        compiler_params=pltpu.CompilerParams(vmem_limit_bytes=mib << 20),
    )(*ins)


def permute(array, axes, pairs):
    return lax.ppermute(array, axes, pairs)


def per_device(tiles, dates, swaths, patch, lead, floor):
    chips = tiles // 2
    relay = chips == 4
    pols = swaths.shape[3]
    swaths, floor = pack(swaths[0]), pack(floor[0])
    blocks = swaths.shape[0]
    rows, subs, _ = floor.shape
    full = (rows, subs, LANES)
    wide = jax.ShapeDtypeStruct(full, F32)
    thin = jax.ShapeDtypeStruct(full, BF16)

    early = 2 if relay else 1
    canvases = 4 * rows * subs * LANES * chips
    early_out, other, own = call(
        functools.partial(place_kernel, relay, chips, early),
        (thin, jax.ShapeDtypeStruct((chips - 1,) + full, BF16), jax.ShapeDtypeStruct((chips,) + full, F32)),
        tuple(pltpu.with_memory_space_constraint(a, pltpu.HBM) for a in (patch[:, 0], lead, swaths)),
        specs=[HBM] * 3,
        mib=(3 * canvases >> 20) + 4,
        scratch=[
            pltpu.VMEM((chips,) + full, F32),
            pltpu.VMEM(swaths.shape, BF16),
            pltpu.SMEM((blocks,), jnp.int32),
            pltpu.SMEM((blocks,), jnp.int32),
            pltpu.SemaphoreType.DMA((blocks + 2,)),
        ],
    )
    partner = [(t, t ^ 1) for t in range(tiles)]
    early_came = permute(early_out, "tile", partner)
    came = permute(other, "tile", partner)
    early_send = call(functools.partial(merge_early_kernel, early), thin, (own, early_came))

    def along(array, moves):
        return permute(array, "tile", [(2 * a + core, 2 * b + core) for a, b in moves for core in range(2)])

    ordered = [s for s in range(chips) if s != early]
    if relay:
        first = along(early_send, [(0, 1), (3, 2), (1, 3), (2, 0)])
    else:
        first = along(early_send, [(c, (c + early) % chips) for c in range(chips)])
    keep, *sends = call(
        functools.partial(merge_kernel, ordered),
        (wide,) + (thin,) * (chips - 2),
        (own, floor, came),
        mib=(2 * canvases >> 20) + 4,
    )
    if relay:
        near_send, far_send = sends
        direct = along(far_send, [(0, 3), (3, 0), (1, 1), (2, 2)])
        near = along(near_send, [(0, 1), (1, 0), (2, 3), (3, 2)])
        passing = call(relay_kernel, thin, (far_send, first))
        passed = along(passing, [(1, 2), (2, 1), (0, 0), (3, 3)])
        arrived = [first, direct, passed, near]
    else:
        arrived = [first]
        for shift, send in zip(ordered[1:], sends):
            arrived.append(along(send, [(c, (c + shift) % chips) for c in range(chips)]))

    half = (rows // 2, subs, LANES)
    wide_half, thin_half = jax.ShapeDtypeStruct(half, F32), jax.ShapeDtypeStruct(half, BF16)
    means, ratio, *sends = call(
        functools.partial(box_kernel, relay, pols),
        (wide, wide, thin_half, thin_half),
        (keep, *arrived),
        mib=8 if relay else 16,
        scratch=[pltpu.VMEM((rows + 2 * STEP, subs, LANES), F32)],
    )

    bits = [1 << b for b in range(dates.bit_length() - 1)]
    starts = (0, rows // 2)
    totals = [ratio, ratio]
    for step in range(len(bits)):
        came = []
        for side in range(2):
            pairs = []
            for d in range(dates):
                for t in range(tiles):
                    bit = bits[step] if (t + side) % 2 == 0 else bits[-1 - step]
                    pairs.append((d * tiles + t, (d ^ bit) * tiles + t))
            came.append(permute(sends[side], ("date", "tile"), pairs))
        if step + 1 < len(bits):
            for side in range(2):
                totals[side], sends[side] = call(
                    functools.partial(add_kernel, starts[side] if step == 0 else 0),
                    (wide_half, thin_half),
                    (totals[side], came[side]),
                    mib=4,
                )
    out = None
    for side in range(2):
        ins = (means, totals[side], came[side]) + (() if out is None else (out,))
        out = call(
            functools.partial(scale_kernel, float(dates), starts[side]),
            thin,
            ins,
            specs=[VMEM] * 3 + [HBM] * (len(ins) - 3),
            out_specs=HBM,
            aliases={3: 0} if len(ins) > 3 else {},
            mib=4,
            scratch=[pltpu.VMEM(half, BF16), pltpu.SemaphoreType.DMA((2,))],
        )
    return unpack(out, pols)[None]


def device_step(tiles, dates, *arrays):
    return per_device(tiles, dates, *arrays)


def solution(mesh):
    return jax.shard_map(
        functools.partial(device_step, mesh.shape["tile"], mesh.shape["date"]),
        mesh=mesh,
        in_specs=(
            P("date", "tile", None, None, None),
            P("tile", None),
            P("tile"),
            P("date", "tile", None, None),
        ),
        out_specs=P("date", "tile", None, None),
        check_vma=False,
    )
```

```python
import functools

import jax
import jax.numpy as jnp
from jax import lax
from jax.experimental import pallas as pl
from jax.experimental.pallas import tpu as pltpu
from jax.sharding import PartitionSpec as P


LANES = 128
REACH = 3
STEP = 8
CUT = 8
VMEM = pl.BlockSpec(memory_space=pltpu.VMEM)
HBM = pl.BlockSpec(memory_space=pltpu.HBM)
F32, BF16 = jnp.float32, jnp.bfloat16


def pack(array):
    *lead, pols, cols = array.shape
    axis = len(lead)
    array = array.reshape(*lead, pols, cols // LANES, LANES)
    return jnp.swapaxes(array, axis, axis + 1).reshape(*lead, pols * cols // LANES, LANES)


def unpack(array, pols):
    *lead, subs, _ = array.shape
    axis = len(lead)
    array = array.reshape(*lead, subs // pols, pols, LANES)
    return jnp.swapaxes(array, axis, axis + 1).reshape(*lead, pols, subs // pols * LANES)


def rows_loop(count, body, unroll=1):
    lax.fori_loop(0, count // STEP, lambda i, c: (body(pl.multiple_of(i * STEP, STEP)), c)[1], 0, unroll=unroll)


def slot_of(relay, chips, owner_chip, chip):
    return owner_chip ^ chip if relay else lax.rem(owner_chip - chip + chips, chips)


def place_kernel(relay, chips, early, owner_hbm, lead_hbm, swath_hbm, *refs):
    early_ref, other_ref, own_ref, acc, swath, owner, lead, sems = refs
    blocks, scan, _, _ = swath.shape
    rows = own_ref.shape[1]
    me = lax.axis_index("tile")
    core, chip = me % 2, me // 2
    small = (
        pltpu.make_async_copy(owner_hbm, owner, sems.at[blocks]),
        pltpu.make_async_copy(lead_hbm, lead, sems.at[blocks + 1]),
    )
    for copy in small:
        copy.start()

    def fetch(block):
        return pltpu.make_async_copy(swath_hbm.at[block], swath.at[block], sems.at[block])

    for block in range(blocks):
        fetch(block).start()

    def clear(at):
        zero = jnp.zeros((STEP,) + acc.shape[2:], F32)
        for slot in range(chips):
            acc[slot, pl.ds(at, STEP)] = zero
            own_ref[slot, pl.ds(at, STEP)] = zero

    rows_loop(rows, clear)
    for copy in small:
        copy.wait()

    def add_into(ref, slot, block, base):
        for row in range(0, scan, STEP):
            span = pl.ds(base + row, STEP)
            ref[slot, span] = ref[slot, span] + swath[block, pl.ds(row, STEP)].astype(F32)

    def insert(block, carry):
        target = owner[block]
        base = lead[block]
        slot = slot_of(relay, chips, target // 2, chip)
        fetch(block).wait()

        @pl.when(target % 2 == core)
        def _():
            add_into(own_ref, slot, block, base)

        @pl.when(target % 2 != core)
        def _():
            add_into(acc, slot, block, base)

        return carry

    lax.fori_loop(0, blocks, insert, 0)
    others = [slot for slot in range(chips) if slot != early]

    def emit(at):
        span = pl.ds(at, STEP)
        early_ref[span] = acc[early, span].astype(BF16)
        for place, slot in enumerate(others):
            other_ref[place, span] = acc[slot, span].astype(BF16)

    rows_loop(rows, emit)


def store_rows(refs, at, value):
    for ref in refs:
        if at < ref.shape[0]:
            ref[pl.ds(at, STEP)] = value.astype(ref.dtype)
            return
        at -= ref.shape[0]


def load_rows(refs, at):
    for ref in refs:
        if at < ref.shape[0]:
            return ref[pl.ds(at, STEP)].astype(F32)
        at -= ref.shape[0]


def merge_early_kernel(early, own_ref, came_ref, *send_refs):
    for at in range(0, came_ref.shape[0], STEP):
        span = pl.ds(at, STEP)
        store_rows(send_refs, at, own_ref[early, span] + came_ref[span].astype(F32))


def merge_kernel(slots, pieces, own_ref, floor_ref, came_ref, keep_ref, *send_refs):
    send_refs = iter(send_refs)
    sends = [[next(send_refs) for _ in range(count)] for count in pieces]
    for at in range(0, keep_ref.shape[0], STEP):
        span = pl.ds(at, STEP)
        for place, slot in enumerate(slots):
            total = own_ref[slot, span] + came_ref[place, span].astype(F32)
            if place:
                store_rows(sends[place - 1], at, total)
            else:
                keep_ref[span] = total + floor_ref[span]


def relay_kernel(start, mine_ref, passing_ref, send_ref):
    for at in range(0, send_ref.shape[0], STEP):
        span = pl.ds(at, STEP)
        total = mine_ref[pl.ds(start + at, STEP)].astype(F32) + passing_ref[span].astype(F32)
        send_ref[span] = total.astype(BF16)


def box_kernel(pieces, pols, first, last, keep_ref, *refs):
    *came_refs, means_ref, ratio_ref, send_ref, canvas = refs
    rows, subs, _ = keep_ref.shape
    low, high = max(first - STEP, 0), min(last + STEP, rows)
    origin = first - STEP
    zero = jnp.zeros((STEP, subs, LANES), F32)
    came = iter(came_refs)
    groups = [[next(came) for _ in range(count)] for count in pieces]
    for at in range(origin, last + STEP, STEP):
        total = zero
        if low <= at < high:
            total = keep_ref[pl.ds(at, STEP)]
            for group in groups:
                total = total + load_rows(group, at)
        canvas[pl.ds(at - origin, STEP)] = total

    shape = (STEP, subs, LANES)
    sub = lax.broadcasted_iota(jnp.int32, shape, 1)
    lane = lax.broadcasted_iota(jnp.int32, shape, 2)
    cols = subs // pols * LANES

    def counted(place, length):
        return jnp.minimum(place + REACH, length - 1) - jnp.maximum(place - REACH, 0) + 1

    col_scale = 1.0 / counted(sub // pols * LANES + lane, cols).astype(F32)

    def ahead(x, by):
        after = jnp.where(sub < subs - pols, pltpu.roll(x, subs - pols, 1), 0.0)
        return pltpu.roll(jnp.where(lane < by, after, x), LANES - by, 2)

    def behind(x, by):
        before = jnp.where(sub >= pols, pltpu.roll(x, pols, 1), 0.0)
        return pltpu.roll(jnp.where(lane >= LANES - by, before, x), by, 2)

    edge_ahead = (sub >= subs - pols) & (lane == LANES - 2)
    edge_behind = (sub < pols) & (lane == 1)

    def box(at, scale):
        x = canvas[pl.ds(at - origin - REACH, STEP + 2 * REACH)]
        two = x[:-1] + x[1:]
        four = two[:-2] + two[2:]
        total = four[:STEP] + two[4 : 4 + STEP] + x[6 : 6 + STEP]
        right, left = ahead(total, 1), behind(total, 1)
        triple = left + total + right
        edge = jnp.where(edge_ahead, right, jnp.where(edge_behind, left, 0.0))
        total = behind(triple, 2) + (total + edge) + ahead(triple, 2)
        means = total * scale
        ratio = x[REACH : REACH + STEP] / means
        span = pl.ds(at - first, STEP)
        means_ref[span] = means
        ratio_ref[span] = ratio
        send_ref[span] = ratio.astype(BF16)

    row = lax.broadcasted_iota(jnp.int32, shape, 0)
    inner = col_scale * (1.0 / (2 * REACH + 1))
    for at in range(first, last, STEP):
        outer = at in (0, rows - STEP)
        scale = col_scale / counted(row + at, rows).astype(F32) if outer else inner
        box(at, scale)


def add_kernel(ratio_ref, came_ref, sum_ref, send_ref):
    def part(at):
        span = pl.ds(at, STEP)
        total = ratio_ref[span] + came_ref[span].astype(F32)
        sum_ref[span] = total
        send_ref[span] = total.astype(BF16)

    rows_loop(sum_ref.shape[0], part, unroll=True)


def scale_kernel(dates, start, means_ref, sum_ref, came_ref, *refs):
    out_hbm, out, sems = refs[-3:]
    rows = sum_ref.shape[0]
    pieces = 2
    size = rows // pieces

    def copy(piece):
        here = pl.ds(piece * size, size)
        return pltpu.make_async_copy(out.at[here], out_hbm.at[pl.ds(start + piece * size, size)], sems.at[piece])

    for piece in range(pieces):
        for at in range(piece * size, piece * size + size, STEP):
            span = pl.ds(at, STEP)
            total = (sum_ref[span] + came_ref[span].astype(F32)) * (1.0 / dates)
            out[span] = (means_ref[span] * total).astype(BF16)
        copy(piece).start()
    for piece in range(pieces):
        copy(piece).wait()


def call(kernel, outs, ins, specs=None, mib=8, scratch=(), out_specs=None, aliases=None):
    return pl.pallas_call(
        kernel,
        out_shape=outs,
        in_specs=specs or [VMEM] * len(ins),
        out_specs=out_specs or jax.tree.map(lambda _: VMEM, outs),
        scratch_shapes=scratch,
        input_output_aliases=aliases or {},
        compiler_params=pltpu.CompilerParams(vmem_limit_bytes=mib << 20),
    )(*ins)


def permute(array, axes, pairs):
    return lax.ppermute(array, axes, pairs)


def per_device(tiles, dates, swaths, patch, lead, floor):
    chips = tiles // 2
    relay = chips == 4
    pols = swaths.shape[3]
    swaths, floor = pack(swaths[0]), pack(floor[0])
    blocks = swaths.shape[0]
    rows, subs, _ = floor.shape
    full = (rows, subs, LANES)
    wide = jax.ShapeDtypeStruct(full, F32)
    thin = jax.ShapeDtypeStruct(full, BF16)

    early = 3 if relay else 1
    slots = [s for s in range(chips) if s != early]
    cut = rows * CUT // 16 // STEP * STEP
    pieces = (cut + STEP, rows - cut - STEP) if relay else (rows,)
    starts = (0, cut + STEP)
    piece_shapes = tuple(jax.ShapeDtypeStruct((size, subs, LANES), BF16) for size in pieces)
    canvases = 4 * rows * subs * LANES * chips
    early_out, other, own = call(
        functools.partial(place_kernel, relay, chips, early),
        (thin, jax.ShapeDtypeStruct((chips - 1,) + full, BF16), jax.ShapeDtypeStruct((chips,) + full, F32)),
        tuple(pltpu.with_memory_space_constraint(a, pltpu.HBM) for a in (patch[:, 0], lead, swaths)),
        specs=[HBM] * 3,
        mib=(3 * canvases >> 20) + 4,
        scratch=[
            pltpu.VMEM((chips,) + full, F32),
            pltpu.VMEM(swaths.shape, BF16),
            pltpu.SMEM((blocks,), jnp.int32),
            pltpu.SMEM((blocks,), jnp.int32),
            pltpu.SemaphoreType.DMA((blocks + 2,)),
        ],
    )
    partner = [(t, t ^ 1) for t in range(tiles)]
    early_came = permute(early_out, "tile", partner)
    came = permute(other, "tile", partner)
    early_sends = call(functools.partial(merge_early_kernel, early), piece_shapes, (own, early_came))

    def along(array, moves):
        return permute(array, "tile", [(2 * a + core, 2 * b + core) for a, b in moves for core in range(2)])

    if relay:
        passing = [along(send, [(c, c ^ 1) for c in range(chips)]) for send in early_sends]
        split = (len(pieces), 1)
        outs = piece_shapes + (thin,)
    else:
        arrived = [[along(early_sends[0], [(c, (c + early) % chips) for c in range(chips)])]]
        split = (1,) * (chips - 2)
        outs = (thin,) * (chips - 2)
    keep, *sends = call(
        functools.partial(merge_kernel, slots, split), (wide,) + outs, (own, floor, came), mib=(2 * canvases >> 20) + 4
    )
    if relay:
        *near_sends, far_send = sends
        far, near = [], []
        for i, passed in enumerate(passing):
            send = call(functools.partial(relay_kernel, starts[i]), piece_shapes[i], (far_send, passed))
            far.append(along(send, [(c, c ^ 2) for c in range(chips)]))
            near.append(along(near_sends[i], [(c, c ^ 1) for c in range(chips)]))
        arrived = [far, near]
    else:
        for shift, send in zip(slots[1:], sends):
            arrived.append([along(send, [(c, (c + shift) % chips) for c in range(chips)])])

    bits = [1 << b for b in range(dates.bit_length() - 1)]
    swaps = []
    for step in range(len(bits)):
        swaps.append([])
        for d in range(dates):
            for t in range(tiles):
                bit = bits[-1 - step] if t % 2 else bits[step]
                swaps[step].append((d * tiles + t, (d ^ bit) * tiles + t))

    out = None
    for first, last in ((0, cut), (cut, rows)):
        shape = (last - first, subs, LANES)
        wide_part, thin_part = jax.ShapeDtypeStruct(shape, F32), jax.ShapeDtypeStruct(shape, BF16)
        used = [group[: 1 if last + STEP <= pieces[0] else None] for group in arrived]
        means, total, send = call(
            functools.partial(box_kernel, tuple(map(len, used)), pols, first, last),
            (wide_part, wide_part, thin_part),
            (keep, *(piece for group in used for piece in group)),
            mib=8 if relay else 16,
            scratch=[pltpu.VMEM((last - first + 2 * STEP, subs, LANES), F32)],
        )
        for step, pairs in enumerate(swaps):
            came = permute(send, ("date", "tile"), pairs)
            if step + 1 < len(swaps):
                total, send = call(add_kernel, (wide_part, thin_part), (total, came), mib=4)
        ins = (means, total, came) + (() if out is None else (out,))
        out = call(
            functools.partial(scale_kernel, float(dates), first),
            thin,
            ins,
            specs=[VMEM] * 3 + [HBM] * (len(ins) - 3),
            out_specs=HBM,
            aliases={3: 0} if len(ins) > 3 else {},
            mib=4,
            scratch=[pltpu.VMEM(shape, BF16), pltpu.SemaphoreType.DMA((2,))],
        )
    return unpack(out, pols)[None]


def device_step(tiles, dates, *arrays):
    return per_device(tiles, dates, *arrays)


def solution(mesh):
    return jax.shard_map(
        functools.partial(device_step, mesh.shape["tile"], mesh.shape["date"]),
        mesh=mesh,
        in_specs=(
            P("date", "tile", None, None, None),
            P("tile", None),
            P("tile"),
            P("date", "tile", None, None),
        ),
        out_specs=P("date", "tile", None, None),
        check_vma=False,
    )
```

```python
import functools

import jax
import jax.numpy as jnp
from jax import lax
from jax.experimental import pallas as pl
from jax.experimental.pallas import tpu as pltpu
from jax.sharding import PartitionSpec as P


LANES = 128
REACH = 3
STEP = 8
CUT = 8
VMEM = pl.BlockSpec(memory_space=pltpu.VMEM)
HBM = pl.BlockSpec(memory_space=pltpu.HBM)
F32, BF16 = jnp.float32, jnp.bfloat16


def pack(array):
    *lead, pols, cols = array.shape
    axis = len(lead)
    array = array.reshape(*lead, pols, cols // LANES, LANES)
    return jnp.swapaxes(array, axis, axis + 1).reshape(*lead, pols * cols // LANES, LANES)


def unpack(array, pols):
    *lead, subs, _ = array.shape
    axis = len(lead)
    array = array.reshape(*lead, subs // pols, pols, LANES)
    return jnp.swapaxes(array, axis, axis + 1).reshape(*lead, pols, subs // pols * LANES)


def rows_loop(count, body, unroll=1):
    lax.fori_loop(0, count // STEP, lambda i, c: (body(pl.multiple_of(i * STEP, STEP)), c)[1], 0, unroll=unroll)


def slot_of(relay, chips, owner_chip, chip):
    return owner_chip ^ chip if relay else lax.rem(owner_chip - chip + chips, chips)


def place_kernel(relay, chips, early, owner_hbm, lead_hbm, swath_hbm, *refs):
    early_ref, other_ref, own_ref, acc, swath, owner, lead, sems = refs
    blocks, scan, _, _ = swath.shape
    rows = own_ref.shape[1]
    me = lax.axis_index("tile")
    core, chip = me % 2, me // 2
    small = (
        pltpu.make_async_copy(owner_hbm, owner, sems.at[blocks]),
        pltpu.make_async_copy(lead_hbm, lead, sems.at[blocks + 1]),
    )
    for copy in small:
        copy.start()

    def fetch(block):
        return pltpu.make_async_copy(swath_hbm.at[block], swath.at[block], sems.at[block])

    for block in range(blocks):
        fetch(block).start()

    def clear(at):
        zero = jnp.zeros((STEP,) + acc.shape[2:], F32)
        for slot in range(chips):
            acc[slot, pl.ds(at, STEP)] = zero
            own_ref[slot, pl.ds(at, STEP)] = zero

    rows_loop(rows, clear)
    for copy in small:
        copy.wait()

    def add_into(ref, slot, block, base):
        for row in range(0, scan, STEP):
            span = pl.ds(base + row, STEP)
            ref[slot, span] = ref[slot, span] + swath[block, pl.ds(row, STEP)].astype(F32)

    def insert(block, carry):
        target = owner[block]
        base = lead[block]
        slot = slot_of(relay, chips, target // 2, chip)
        fetch(block).wait()

        @pl.when(target % 2 == core)
        def _():
            add_into(own_ref, slot, block, base)

        @pl.when(target % 2 != core)
        def _():
            add_into(acc, slot, block, base)

        return carry

    lax.fori_loop(0, blocks, insert, 0)
    others = [slot for slot in range(chips) if slot != early]

    def emit(at):
        span = pl.ds(at, STEP)
        early_ref[span] = acc[early, span].astype(BF16)
        for place, slot in enumerate(others):
            other_ref[place, span] = acc[slot, span].astype(BF16)

    rows_loop(rows, emit)


def store_rows(refs, at, value):
    for ref in refs:
        if at < ref.shape[0]:
            ref[pl.ds(at, STEP)] = value.astype(ref.dtype)
            return
        at -= ref.shape[0]


def load_rows(refs, at):
    for ref in refs:
        if at < ref.shape[0]:
            return ref[pl.ds(at, STEP)].astype(F32)
        at -= ref.shape[0]


def merge_early_kernel(early, own_ref, came_ref, *send_refs):
    for at in range(0, came_ref.shape[0], STEP):
        span = pl.ds(at, STEP)
        store_rows(send_refs, at, own_ref[early, span] + came_ref[span].astype(F32))


def merge_kernel(slots, pieces, own_ref, floor_ref, came_ref, keep_ref, *send_refs):
    send_refs = iter(send_refs)
    sends = [[next(send_refs) for _ in range(count)] for count in pieces]
    for at in range(0, keep_ref.shape[0], STEP):
        span = pl.ds(at, STEP)
        for place, slot in enumerate(slots):
            total = own_ref[slot, span] + came_ref[place, span].astype(F32)
            if place:
                store_rows(sends[place - 1], at, total)
            else:
                keep_ref[span] = total + floor_ref[span]


def relay_kernel(start, mine_ref, passing_ref, *refs):
    send_ref = refs[-1] if start else refs[0]
    if not start:
        refs[1][...] = jnp.zeros(refs[1].shape, BF16)
    for at in range(0, send_ref.shape[0], STEP):
        span = pl.ds(at, STEP)
        total = mine_ref[pl.ds(start + at, STEP)].astype(F32) + passing_ref[span].astype(F32)
        send_ref[span] = total.astype(BF16)


def box_kernel(pieces, pols, first, last, keep_ref, *refs):
    *came_refs, means_ref, ratio_ref, send_ref, canvas = refs
    rows, subs, _ = keep_ref.shape
    low, high = max(first - STEP, 0), min(last + STEP, rows)
    origin = first - STEP
    zero = jnp.zeros((STEP, subs, LANES), F32)
    came = iter(came_refs)
    groups = [[next(came) for _ in range(count)] for count in pieces]
    for at in range(origin, last + STEP, STEP):
        total = zero
        if low <= at < high:
            total = keep_ref[pl.ds(at, STEP)]
            for group in groups:
                total = total + load_rows(group, at)
        canvas[pl.ds(at - origin, STEP)] = total

    shape = (STEP, subs, LANES)
    sub = lax.broadcasted_iota(jnp.int32, shape, 1)
    lane = lax.broadcasted_iota(jnp.int32, shape, 2)
    cols = subs // pols * LANES

    def counted(place, length):
        return jnp.minimum(place + REACH, length - 1) - jnp.maximum(place - REACH, 0) + 1

    col_scale = 1.0 / counted(sub // pols * LANES + lane, cols).astype(F32)

    def ahead(x, by):
        after = jnp.where(sub < subs - pols, pltpu.roll(x, subs - pols, 1), 0.0)
        return pltpu.roll(jnp.where(lane < by, after, x), LANES - by, 2)

    def behind(x, by):
        before = jnp.where(sub >= pols, pltpu.roll(x, pols, 1), 0.0)
        return pltpu.roll(jnp.where(lane >= LANES - by, before, x), by, 2)

    edge_ahead = (sub >= subs - pols) & (lane == LANES - 2)
    edge_behind = (sub < pols) & (lane == 1)

    def box(at, scale):
        x = canvas[pl.ds(at - origin - REACH, STEP + 2 * REACH)]
        two = x[:-1] + x[1:]
        four = two[:-2] + two[2:]
        total = four[:STEP] + two[4 : 4 + STEP] + x[6 : 6 + STEP]
        right, left = ahead(total, 1), behind(total, 1)
        triple = left + total + right
        edge = jnp.where(edge_ahead, right, jnp.where(edge_behind, left, 0.0))
        total = behind(triple, 2) + (total + edge) + ahead(triple, 2)
        means = total * scale
        ratio = x[REACH : REACH + STEP] / means
        span = pl.ds(at - first, STEP)
        means_ref[span] = means
        ratio_ref[span] = ratio
        send_ref[span] = ratio.astype(BF16)

    row = lax.broadcasted_iota(jnp.int32, shape, 0)
    inner = col_scale * (1.0 / (2 * REACH + 1))
    for at in range(first, last, STEP):
        outer = at in (0, rows - STEP)
        scale = col_scale / counted(row + at, rows).astype(F32) if outer else inner
        box(at, scale)


def add_kernel(ratio_ref, came_ref, sum_ref, send_ref):
    def part(at):
        span = pl.ds(at, STEP)
        total = ratio_ref[span] + came_ref[span].astype(F32)
        sum_ref[span] = total
        send_ref[span] = total.astype(BF16)

    rows_loop(sum_ref.shape[0], part, unroll=True)


def scale_kernel(dates, start, means_ref, sum_ref, came_ref, *refs):
    out_hbm, out, sems = refs[-3:]
    rows = sum_ref.shape[0]
    pieces = 2
    size = rows // pieces

    def copy(piece):
        here = pl.ds(piece * size, size)
        return pltpu.make_async_copy(out.at[here], out_hbm.at[pl.ds(start + piece * size, size)], sems.at[piece])

    for piece in range(pieces):
        for at in range(piece * size, piece * size + size, STEP):
            span = pl.ds(at, STEP)
            total = (sum_ref[span] + came_ref[span].astype(F32)) * (1.0 / dates)
            out[span] = (means_ref[span] * total).astype(BF16)
        copy(piece).start()
    for piece in range(pieces):
        copy(piece).wait()


def call(kernel, outs, ins, specs=None, mib=8, scratch=(), out_specs=None, aliases=None):
    return pl.pallas_call(
        kernel,
        out_shape=outs,
        in_specs=specs or [VMEM] * len(ins),
        out_specs=out_specs or jax.tree.map(lambda _: VMEM, outs),
        scratch_shapes=scratch,
        input_output_aliases=aliases or {},
        compiler_params=pltpu.CompilerParams(vmem_limit_bytes=mib << 20),
    )(*ins)


def permute(array, axes, pairs):
    return lax.ppermute(array, axes, pairs)


def per_device(tiles, dates, swaths, patch, lead, floor):
    chips = tiles // 2
    relay = chips == 4
    pols = swaths.shape[3]
    swaths, floor = pack(swaths[0]), pack(floor[0])
    blocks = swaths.shape[0]
    rows, subs, _ = floor.shape
    full = (rows, subs, LANES)
    wide = jax.ShapeDtypeStruct(full, F32)
    thin = jax.ShapeDtypeStruct(full, BF16)

    early = 3 if relay else 1
    slots = [s for s in range(chips) if s != early]
    cut = rows * CUT // 16 // STEP * STEP
    pieces = (cut + STEP, rows - cut - STEP) if relay else (rows,)
    starts = (0, cut + STEP)
    piece_shapes = tuple(jax.ShapeDtypeStruct((size, subs, LANES), BF16) for size in pieces)
    canvases = 4 * rows * subs * LANES * chips
    early_out, other, own = call(
        functools.partial(place_kernel, relay, chips, early),
        (thin, jax.ShapeDtypeStruct((chips - 1,) + full, BF16), jax.ShapeDtypeStruct((chips,) + full, F32)),
        tuple(pltpu.with_memory_space_constraint(a, pltpu.HBM) for a in (patch[:, 0], lead, swaths)),
        specs=[HBM] * 3,
        mib=(3 * canvases >> 20) + 4,
        scratch=[
            pltpu.VMEM((chips,) + full, F32),
            pltpu.VMEM(swaths.shape, BF16),
            pltpu.SMEM((blocks,), jnp.int32),
            pltpu.SMEM((blocks,), jnp.int32),
            pltpu.SemaphoreType.DMA((blocks + 2,)),
        ],
    )
    partner = [(t, t ^ 1) for t in range(tiles)]
    early_came = permute(early_out, "tile", partner)
    came = permute(other, "tile", partner)
    early_sends = call(functools.partial(merge_early_kernel, early), piece_shapes, (own, early_came))

    def along(array, moves):
        return permute(array, "tile", [(2 * a + core, 2 * b + core) for a, b in moves for core in range(2)])

    if relay:
        passing = [along(send, [(c, c ^ 1) for c in range(chips)]) for send in early_sends]
        split = (len(pieces), 1)
        outs = piece_shapes + (thin,)
    else:
        arrived = [[along(early_sends[0], [(c, (c + early) % chips) for c in range(chips)])]]
        split = (1,) * (chips - 2)
        outs = (thin,) * (chips - 2)
    keep, *sends = call(
        functools.partial(merge_kernel, slots, split), (wide,) + outs, (own, floor, came), mib=(2 * canvases >> 20) + 4
    )
    if relay:
        *near_sends, far_send = sends
        far, near = [], []
        ready = jax.ShapeDtypeStruct((1, subs, LANES), BF16)
        waits = ()
        for i, passed in enumerate(passing):
            send, *ready_out = call(
                functools.partial(relay_kernel, starts[i]),
                (piece_shapes[i],) + (ready,) * (i == 0),
                (far_send, passed, *waits),
            )
            far.append(along(send, [(c, c ^ 2) for c in range(chips)]))
            near.append(along(near_sends[i], [(c, c ^ 1) for c in range(chips)]))
            if i == 0:
                waits = (permute(ready_out[0], "tile", partner),)
        arrived = [far, near]
    else:
        for shift, send in zip(slots[1:], sends):
            arrived.append([along(send, [(c, (c + shift) % chips) for c in range(chips)])])

    bits = [1 << b for b in range(dates.bit_length() - 1)]

    def across(step, part):
        pairs = []
        for d in range(dates):
            for t in range(tiles):
                bit = bits[-1 - step] if (t + part) % 2 else bits[step]
                pairs.append((d * tiles + t, (d ^ bit) * tiles + t))
        return pairs

    out = None
    for part, (first, last) in enumerate(((0, cut), (cut, rows))):
        shape = (last - first, subs, LANES)
        wide_part, thin_part = jax.ShapeDtypeStruct(shape, F32), jax.ShapeDtypeStruct(shape, BF16)
        used = [group[: 1 if last + STEP <= pieces[0] else None] for group in arrived]
        means, total, send = call(
            functools.partial(box_kernel, tuple(map(len, used)), pols, first, last),
            (wide_part, wide_part, thin_part),
            (keep, *(piece for group in used for piece in group)),
            mib=8 if relay else 16,
            scratch=[pltpu.VMEM((last - first + 2 * STEP, subs, LANES), F32)],
        )
        for step in range(len(bits)):
            came = permute(send, ("date", "tile"), across(step, part))
            if step + 1 < len(bits):
                total, send = call(add_kernel, (wide_part, thin_part), (total, came), mib=4)
        ins = (means, total, came) + (() if out is None else (out,))
        out = call(
            functools.partial(scale_kernel, float(dates), first),
            thin,
            ins,
            specs=[VMEM] * 3 + [HBM] * (len(ins) - 3),
            out_specs=HBM,
            aliases={3: 0} if len(ins) > 3 else {},
            mib=4,
            scratch=[pltpu.VMEM(shape, BF16), pltpu.SemaphoreType.DMA((2,))],
        )
    return unpack(out, pols)[None]


def device_step(tiles, dates, *arrays):
    return per_device(tiles, dates, *arrays)


def solution(mesh):
    return jax.shard_map(
        functools.partial(device_step, mesh.shape["tile"], mesh.shape["date"]),
        mesh=mesh,
        in_specs=(
            P("date", "tile", None, None, None),
            P("tile", None),
            P("tile"),
            P("date", "tile", None, None),
        ),
        out_specs=P("date", "tile", None, None),
        check_vma=False,
    )
```

```python
import functools

import jax
import jax.numpy as jnp
from jax import lax
from jax.experimental import pallas as pl
from jax.experimental.pallas import tpu as pltpu
from jax.sharding import PartitionSpec as P


LANES = 128
REACH = 3
STEP = 8
CUT = 8
VMEM = pl.BlockSpec(memory_space=pltpu.VMEM)
HBM = pl.BlockSpec(memory_space=pltpu.HBM)
F32, BF16 = jnp.float32, jnp.bfloat16


def pack(array):
    *lead, pols, cols = array.shape
    axis = len(lead)
    array = array.reshape(*lead, pols, cols // LANES, LANES)
    return jnp.swapaxes(array, axis, axis + 1).reshape(*lead, pols * cols // LANES, LANES)


def unpack(array, pols):
    *lead, subs, _ = array.shape
    axis = len(lead)
    array = array.reshape(*lead, subs // pols, pols, LANES)
    return jnp.swapaxes(array, axis, axis + 1).reshape(*lead, pols, subs // pols * LANES)


def rows_loop(count, body, unroll=1):
    lax.fori_loop(0, count // STEP, lambda i, c: (body(pl.multiple_of(i * STEP, STEP)), c)[1], 0, unroll=unroll)


def slot_of(relay, chips, owner_chip, chip):
    return owner_chip ^ chip if relay else lax.rem(owner_chip - chip + chips, chips)


def place_kernel(relay, chips, early, owner_hbm, lead_hbm, swath_hbm, *refs):
    early_ref, acc, own_ref, swath, owner, lead, sems = refs
    blocks, scan, _, _ = swath.shape
    rows = own_ref.shape[1]
    me = lax.axis_index("tile")
    core, chip = me % 2, me // 2
    small = (
        pltpu.make_async_copy(owner_hbm, owner, sems.at[blocks]),
        pltpu.make_async_copy(lead_hbm, lead, sems.at[blocks + 1]),
    )
    for copy in small:
        copy.start()

    def fetch(block):
        return pltpu.make_async_copy(swath_hbm.at[block], swath.at[block], sems.at[block])

    for block in range(blocks):
        fetch(block).start()

    def clear(at):
        zero = jnp.zeros((STEP,) + acc.shape[2:], F32)
        for slot in range(chips):
            acc[slot, pl.ds(at, STEP)] = zero
            own_ref[slot, pl.ds(at, STEP)] = zero

    rows_loop(rows, clear)
    for copy in small:
        copy.wait()

    def add_into(ref, slot, block, base):
        for row in range(0, scan, STEP):
            span = pl.ds(base + row, STEP)
            ref[slot, span] = ref[slot, span] + swath[block, pl.ds(row, STEP)].astype(F32)

    def insert(block, carry):
        target = owner[block]
        base = lead[block]
        slot = slot_of(relay, chips, target // 2, chip)
        fetch(block).wait()

        @pl.when(target % 2 == core)
        def _():
            add_into(own_ref, slot, block, base)

        @pl.when(target % 2 != core)
        def _():
            add_into(acc, slot, block, base)

        return carry

    lax.fori_loop(0, blocks, insert, 0)
    for at in range(0, early_ref.shape[0], STEP):
        early_ref[pl.ds(at, STEP)] = acc[early, pl.ds(at, STEP)].astype(BF16)


def round_kernel(slots, early, acc, rest_ref):
    rows = acc.shape[1]

    def part(at):
        for place, slot in enumerate(slots):
            rest_ref[pl.ds(place * rows + at, STEP)] = acc[slot, pl.ds(at, STEP)].astype(BF16)

    rows_loop(rows, part)
    base = len(slots) * rows
    skipped = rows - (rest_ref.shape[0] - base)
    for at in range(skipped, rows, STEP):
        rest_ref[pl.ds(base + at - skipped, STEP)] = acc[early, pl.ds(at, STEP)].astype(BF16)


def store_rows(refs, at, value):
    for ref in refs:
        if at < ref.shape[0]:
            ref[pl.ds(at, STEP)] = value.astype(ref.dtype)
            return
        at -= ref.shape[0]


def load_rows(refs, at):
    for ref in refs:
        if at < ref.shape[0]:
            return ref[pl.ds(at, STEP)].astype(F32)
        at -= ref.shape[0]


def merge_early_kernel(early, own_ref, came_ref, send_ref):
    for at in range(0, send_ref.shape[0], STEP):
        span = pl.ds(at, STEP)
        send_ref[span] = (own_ref[early, span] + came_ref[span].astype(F32)).astype(BF16)


def merge_kernel(slots, early, pieces, own_ref, floor_ref, came_ref, keep_ref, *send_refs):
    send_refs = iter(send_refs)
    sends = [[next(send_refs) for _ in range(count)] for count in pieces]
    rows = keep_ref.shape[0]
    base = len(slots) * rows
    skipped = rows - (came_ref.shape[0] - base)
    for at in range(0, rows, STEP):
        span = pl.ds(at, STEP)
        if at >= skipped:
            total = own_ref[early, span] + came_ref[pl.ds(base + at - skipped, STEP)].astype(F32)
            sends[-1][0][pl.ds(at - skipped, STEP)] = total.astype(BF16)
        for place, slot in enumerate(slots):
            total = own_ref[slot, span] + came_ref[pl.ds(place * rows + at, STEP)].astype(F32)
            if place:
                store_rows(sends[place - 1], at, total)
            else:
                keep_ref[span] = total + floor_ref[span]


def relay_kernel(start, mine_ref, passing_ref, *refs):
    send_ref = refs[-1] if start else refs[0]
    if not start:
        refs[1][...] = jnp.zeros(refs[1].shape, BF16)
    for at in range(0, send_ref.shape[0], STEP):
        span = pl.ds(at, STEP)
        total = mine_ref[pl.ds(start + at, STEP)].astype(F32) + passing_ref[span].astype(F32)
        send_ref[span] = total.astype(BF16)


def box_kernel(pieces, pols, first, last, keep_ref, *refs):
    *came_refs, means_ref, ratio_ref, send_ref, canvas = refs
    rows, subs, _ = keep_ref.shape
    low, high = max(first - STEP, 0), min(last + STEP, rows)
    origin = first - STEP
    zero = jnp.zeros((STEP, subs, LANES), F32)
    came = iter(came_refs)
    groups = [[next(came) for _ in range(count)] for count in pieces]
    for at in range(origin, last + STEP, STEP):
        total = zero
        if low <= at < high:
            total = keep_ref[pl.ds(at, STEP)]
            for group in groups:
                total = total + load_rows(group, at)
        canvas[pl.ds(at - origin, STEP)] = total

    shape = (STEP, subs, LANES)
    sub = lax.broadcasted_iota(jnp.int32, shape, 1)
    lane = lax.broadcasted_iota(jnp.int32, shape, 2)
    cols = subs // pols * LANES

    def counted(place, length):
        return jnp.minimum(place + REACH, length - 1) - jnp.maximum(place - REACH, 0) + 1

    col_scale = 1.0 / counted(sub // pols * LANES + lane, cols).astype(F32)

    def ahead(x, by):
        after = jnp.where(sub < subs - pols, pltpu.roll(x, subs - pols, 1), 0.0)
        return pltpu.roll(jnp.where(lane < by, after, x), LANES - by, 2)

    def behind(x, by):
        before = jnp.where(sub >= pols, pltpu.roll(x, pols, 1), 0.0)
        return pltpu.roll(jnp.where(lane >= LANES - by, before, x), by, 2)

    edge_ahead = (sub >= subs - pols) & (lane == LANES - 2)
    edge_behind = (sub < pols) & (lane == 1)

    def box(at, scale):
        x = canvas[pl.ds(at - origin - REACH, STEP + 2 * REACH)]
        two = x[:-1] + x[1:]
        four = two[:-2] + two[2:]
        total = four[:STEP] + two[4 : 4 + STEP] + x[6 : 6 + STEP]
        right, left = ahead(total, 1), behind(total, 1)
        triple = left + total + right
        edge = jnp.where(edge_ahead, right, jnp.where(edge_behind, left, 0.0))
        total = behind(triple, 2) + (total + edge) + ahead(triple, 2)
        means = total * scale
        ratio = x[REACH : REACH + STEP] / means
        span = pl.ds(at - first, STEP)
        means_ref[span] = means
        ratio_ref[span] = ratio
        send_ref[span] = ratio.astype(BF16)

    row = lax.broadcasted_iota(jnp.int32, shape, 0)
    inner = col_scale * (1.0 / (2 * REACH + 1))
    for at in range(first, last, STEP):
        outer = at in (0, rows - STEP)
        scale = col_scale / counted(row + at, rows).astype(F32) if outer else inner
        box(at, scale)


def add_kernel(ratio_ref, came_ref, sum_ref, send_ref):
    def part(at):
        span = pl.ds(at, STEP)
        total = ratio_ref[span] + came_ref[span].astype(F32)
        sum_ref[span] = total
        send_ref[span] = total.astype(BF16)

    rows_loop(sum_ref.shape[0], part, unroll=True)


def scale_kernel(dates, start, means_ref, sum_ref, came_ref, *refs):
    out_hbm, out, sems = refs[-3:]
    rows = sum_ref.shape[0]
    pieces = 2
    size = rows // pieces

    def copy(piece):
        here = pl.ds(piece * size, size)
        return pltpu.make_async_copy(out.at[here], out_hbm.at[pl.ds(start + piece * size, size)], sems.at[piece])

    for piece in range(pieces):
        for at in range(piece * size, piece * size + size, STEP):
            span = pl.ds(at, STEP)
            total = (sum_ref[span] + came_ref[span].astype(F32)) * (1.0 / dates)
            out[span] = (means_ref[span] * total).astype(BF16)
        copy(piece).start()
    for piece in range(pieces):
        copy(piece).wait()


def call(kernel, outs, ins, specs=None, mib=8, scratch=(), out_specs=None, aliases=None):
    return pl.pallas_call(
        kernel,
        out_shape=outs,
        in_specs=specs or [VMEM] * len(ins),
        out_specs=out_specs or jax.tree.map(lambda _: VMEM, outs),
        scratch_shapes=scratch,
        input_output_aliases=aliases or {},
        compiler_params=pltpu.CompilerParams(vmem_limit_bytes=mib << 20),
    )(*ins)


def permute(array, axes, pairs):
    return lax.ppermute(array, axes, pairs)


def per_device(tiles, dates, swaths, patch, lead, floor):
    chips = tiles // 2
    relay = chips == 4
    pols = swaths.shape[3]
    swaths, floor = pack(swaths[0]), pack(floor[0])
    blocks = swaths.shape[0]
    rows, subs, _ = floor.shape
    full = (rows, subs, LANES)
    wide = jax.ShapeDtypeStruct(full, F32)
    thin = jax.ShapeDtypeStruct(full, BF16)

    early = 3 if relay else 1
    slots = [s for s in range(chips) if s != early]
    cut = rows * CUT // 16 // STEP * STEP
    pieces = (cut + STEP, rows - cut - STEP) if relay else (rows,)
    starts = (0, cut + STEP)
    piece_shapes = tuple(jax.ShapeDtypeStruct((size, subs, LANES), BF16) for size in pieces)
    canvases = 4 * rows * subs * LANES * chips
    canvas_shape = jax.ShapeDtypeStruct((chips,) + full, F32)
    early_out, acc, own = call(
        functools.partial(place_kernel, relay, chips, early),
        (piece_shapes[0], canvas_shape, canvas_shape),
        tuple(pltpu.with_memory_space_constraint(a, pltpu.HBM) for a in (patch[:, 0], lead, swaths)),
        specs=[HBM] * 3,
        mib=(2 * canvases >> 20) + 4,
        scratch=[
            pltpu.VMEM(swaths.shape, BF16),
            pltpu.SMEM((blocks,), jnp.int32),
            pltpu.SMEM((blocks,), jnp.int32),
            pltpu.SemaphoreType.DMA((blocks + 2,)),
        ],
    )
    partner = [(t, t ^ 1) for t in range(tiles)]
    came_early = permute(early_out, "tile", partner)
    rest = call(
        functools.partial(round_kernel, slots, early),
        jax.ShapeDtypeStruct((chips * rows - pieces[0], subs, LANES), BF16),
        (acc,),
        mib=(2 * canvases >> 20) + 4,
    )
    came = permute(rest, "tile", partner)
    early_send = call(functools.partial(merge_early_kernel, early), piece_shapes[0], (own, came_early))

    def along(array, moves):
        return permute(array, "tile", [(2 * a + core, 2 * b + core) for a, b in moves for core in range(2)])

    shift = 1 if relay else early
    first_pass = [(c, c ^ shift if relay else (c + shift) % chips) for c in range(chips)]
    passing = [along(early_send, first_pass)]
    if relay:
        split = (2, 1, 1)
        outs = piece_shapes + (thin, piece_shapes[1])
    else:
        split = (1,) * (chips - 2)
        outs = (thin,) * (chips - 2)
    keep, *sends = call(
        functools.partial(merge_kernel, slots, early, split),
        (wide,) + outs,
        (own, floor, came),
        mib=(2 * canvases >> 20) + 4,
    )
    if relay:
        *near_sends, far_send, late_send = sends
        passing.append(along(late_send, first_pass))
        far, near = [], []
        ready = jax.ShapeDtypeStruct((1, subs, LANES), BF16)
        waits = ()
        for i, passed in enumerate(passing):
            send, *ready_out = call(
                functools.partial(relay_kernel, starts[i]),
                (piece_shapes[i],) + (ready,) * (i == 0),
                (far_send, passed, *waits),
            )
            far.append(along(send, [(c, c ^ 2) for c in range(chips)]))
            near.append(along(near_sends[i], [(c, c ^ 1) for c in range(chips)]))
            if i == 0:
                waits = (permute(ready_out[0], "tile", partner),)
        arrived = [far, near]
    else:
        arrived = [passing]
        for shift, send in zip(slots[1:], sends):
            arrived.append([along(send, [(c, (c + shift) % chips) for c in range(chips)])])

    bits = [1 << b for b in range(dates.bit_length() - 1)]

    def across(step, part):
        pairs = []
        for d in range(dates):
            for t in range(tiles):
                bit = bits[-1 - step] if (t + part) % 2 else bits[step]
                pairs.append((d * tiles + t, (d ^ bit) * tiles + t))
        return pairs

    out = None
    for part, (first, last) in enumerate(((0, cut), (cut, rows))):
        shape = (last - first, subs, LANES)
        wide_part, thin_part = jax.ShapeDtypeStruct(shape, F32), jax.ShapeDtypeStruct(shape, BF16)
        used = [group[: 1 if last + STEP <= pieces[0] else None] for group in arrived]
        means, total, send = call(
            functools.partial(box_kernel, tuple(map(len, used)), pols, first, last),
            (wide_part, wide_part, thin_part),
            (keep, *(piece for group in used for piece in group)),
            mib=8 if relay else 16,
            scratch=[pltpu.VMEM((last - first + 2 * STEP, subs, LANES), F32)],
        )
        for step in range(len(bits)):
            came = permute(send, ("date", "tile"), across(step, part))
            if step + 1 < len(bits):
                total, send = call(add_kernel, (wide_part, thin_part), (total, came), mib=4)
        ins = (means, total, came) + (() if out is None else (out,))
        out = call(
            functools.partial(scale_kernel, float(dates), first),
            thin,
            ins,
            specs=[VMEM] * 3 + [HBM] * (len(ins) - 3),
            out_specs=HBM,
            aliases={3: 0} if len(ins) > 3 else {},
            mib=4,
            scratch=[pltpu.VMEM(shape, BF16), pltpu.SemaphoreType.DMA((2,))],
        )
    return unpack(out, pols)[None]


def device_step(tiles, dates, *arrays):
    return per_device(tiles, dates, *arrays)


def solution(mesh):
    return jax.shard_map(
        functools.partial(device_step, mesh.shape["tile"], mesh.shape["date"]),
        mesh=mesh,
        in_specs=(
            P("date", "tile", None, None, None),
            P("tile", None),
            P("tile"),
            P("date", "tile", None, None),
        ),
        out_specs=P("date", "tile", None, None),
        check_vma=False,
    )
```

```python
import functools

import jax
import jax.numpy as jnp
from jax import lax
from jax.experimental import pallas as pl
from jax.experimental.pallas import tpu as pltpu
from jax.sharding import PartitionSpec as P


LANES = 128
REACH = 3
STEP = 8
CUT = 8
VMEM = pl.BlockSpec(memory_space=pltpu.VMEM)
HBM = pl.BlockSpec(memory_space=pltpu.HBM)
F32, BF16 = jnp.float32, jnp.bfloat16


def pack(array):
    *lead, pols, cols = array.shape
    axis = len(lead)
    array = array.reshape(*lead, pols, cols // LANES, LANES)
    return jnp.swapaxes(array, axis, axis + 1).reshape(*lead, pols * cols // LANES, LANES)


def unpack(array, pols):
    *lead, subs, _ = array.shape
    axis = len(lead)
    array = array.reshape(*lead, subs // pols, pols, LANES)
    return jnp.swapaxes(array, axis, axis + 1).reshape(*lead, pols, subs // pols * LANES)


def rows_loop(count, body, unroll=1):
    lax.fori_loop(0, count // STEP, lambda i, c: (body(pl.multiple_of(i * STEP, STEP)), c)[1], 0, unroll=unroll)


def slot_of(relay, chips, owner_chip, chip):
    return owner_chip ^ chip if relay else lax.rem(owner_chip - chip + chips, chips)


def place_kernel(relay, chips, early, owner_hbm, lead_hbm, swath_hbm, *refs):
    early_ref, acc, own_ref, swath, owner, lead, sems = refs
    blocks, scan, _, _ = swath.shape
    rows = own_ref.shape[1]
    me = lax.axis_index("tile")
    core, chip = me % 2, me // 2
    small = (
        pltpu.make_async_copy(owner_hbm, owner, sems.at[blocks]),
        pltpu.make_async_copy(lead_hbm, lead, sems.at[blocks + 1]),
    )
    for copy in small:
        copy.start()

    def fetch(block):
        return pltpu.make_async_copy(swath_hbm.at[block], swath.at[block], sems.at[block])

    for block in range(blocks):
        fetch(block).start()

    def clear(at):
        zero = jnp.zeros((STEP,) + acc.shape[2:], F32)
        for slot in range(chips):
            acc[slot, pl.ds(at, STEP)] = zero
            own_ref[slot, pl.ds(at, STEP)] = zero

    rows_loop(rows, clear)
    for copy in small:
        copy.wait()

    def add_into(ref, slot, block, base):
        for row in range(0, scan, STEP):
            span = pl.ds(base + row, STEP)
            ref[slot, span] = ref[slot, span] + swath[block, pl.ds(row, STEP)].astype(F32)

    def insert(block, carry):
        target = owner[block]
        base = lead[block]
        slot = slot_of(relay, chips, target // 2, chip)
        fetch(block).wait()

        @pl.when(target % 2 == core)
        def _():
            add_into(own_ref, slot, block, base)

        @pl.when(target % 2 != core)
        def _():
            add_into(acc, slot, block, base)

        return carry

    lax.fori_loop(0, blocks, insert, 0)
    for at in range(0, early_ref.shape[0], STEP):
        early_ref[pl.ds(at, STEP)] = acc[early, pl.ds(at, STEP)].astype(BF16)


def round_kernel(slots, early, acc, rest_ref):
    rows = acc.shape[1]

    def part(at):
        for place, slot in enumerate(slots):
            rest_ref[pl.ds(place * rows + at, STEP)] = acc[slot, pl.ds(at, STEP)].astype(BF16)

    rows_loop(rows, part)
    base = len(slots) * rows
    skipped = rows - (rest_ref.shape[0] - base)
    for at in range(skipped, rows, STEP):
        rest_ref[pl.ds(base + at - skipped, STEP)] = acc[early, pl.ds(at, STEP)].astype(BF16)


def store_rows(refs, at, value):
    for ref in refs:
        if at < ref.shape[0]:
            ref[pl.ds(at, STEP)] = value.astype(ref.dtype)
            return
        at -= ref.shape[0]


def load_rows(refs, at):
    for ref in refs:
        if at < ref.shape[0]:
            return ref[pl.ds(at, STEP)].astype(F32)
        at -= ref.shape[0]


def merge_early_kernel(early, own_ref, came_ref, send_ref):
    for at in range(0, send_ref.shape[0], STEP):
        span = pl.ds(at, STEP)
        send_ref[span] = (own_ref[early, span] + came_ref[span].astype(F32)).astype(BF16)


def merge_kernel(slots, early, pieces, own_ref, floor_ref, came_ref, keep_ref, *send_refs):
    send_refs = iter(send_refs)
    sends = [[next(send_refs) for _ in range(count)] for count in pieces]
    rows = keep_ref.shape[0]
    base = len(slots) * rows
    skipped = rows - (came_ref.shape[0] - base)
    for at in range(0, rows, STEP):
        span = pl.ds(at, STEP)
        if at >= skipped:
            total = own_ref[early, span] + came_ref[pl.ds(base + at - skipped, STEP)].astype(F32)
            sends[-1][0][pl.ds(at - skipped, STEP)] = total.astype(BF16)
        for place, slot in enumerate(slots):
            total = own_ref[slot, span] + came_ref[pl.ds(place * rows + at, STEP)].astype(F32)
            if place:
                store_rows(sends[place - 1], at, total)
            else:
                keep_ref[span] = total + floor_ref[span]


def relay_kernel(start, mine_ref, passing_ref, send_ref):
    for at in range(0, send_ref.shape[0], STEP):
        span = pl.ds(at, STEP)
        total = mine_ref[pl.ds(start + at, STEP)].astype(F32) + passing_ref[span].astype(F32)
        send_ref[span] = total.astype(BF16)


def box_kernel(pieces, pols, first, last, keep_ref, *refs):
    *came_refs, means_ref, ratio_ref, send_ref, canvas = refs
    rows, subs, _ = keep_ref.shape
    low, high = max(first - STEP, 0), min(last + STEP, rows)
    origin = first - STEP
    zero = jnp.zeros((STEP, subs, LANES), F32)
    came = iter(came_refs)
    groups = [[next(came) for _ in range(count)] for count in pieces]
    for at in range(origin, last + STEP, STEP):
        total = zero
        if low <= at < high:
            total = keep_ref[pl.ds(at, STEP)]
            for group in groups:
                total = total + load_rows(group, at)
        canvas[pl.ds(at - origin, STEP)] = total

    shape = (STEP, subs, LANES)
    sub = lax.broadcasted_iota(jnp.int32, shape, 1)
    lane = lax.broadcasted_iota(jnp.int32, shape, 2)
    cols = subs // pols * LANES

    def counted(place, length):
        return jnp.minimum(place + REACH, length - 1) - jnp.maximum(place - REACH, 0) + 1

    col_scale = 1.0 / counted(sub // pols * LANES + lane, cols).astype(F32)

    def ahead(x, by):
        after = jnp.where(sub < subs - pols, pltpu.roll(x, subs - pols, 1), 0.0)
        return pltpu.roll(jnp.where(lane < by, after, x), LANES - by, 2)

    def behind(x, by):
        before = jnp.where(sub >= pols, pltpu.roll(x, pols, 1), 0.0)
        return pltpu.roll(jnp.where(lane >= LANES - by, before, x), by, 2)

    edge_ahead = (sub >= subs - pols) & (lane == LANES - 2)
    edge_behind = (sub < pols) & (lane == 1)

    def box(at, scale):
        x = canvas[pl.ds(at - origin - REACH, STEP + 2 * REACH)]
        two = x[:-1] + x[1:]
        four = two[:-2] + two[2:]
        total = four[:STEP] + two[4 : 4 + STEP] + x[6 : 6 + STEP]
        right, left = ahead(total, 1), behind(total, 1)
        triple = left + total + right
        edge = jnp.where(edge_ahead, right, jnp.where(edge_behind, left, 0.0))
        total = behind(triple, 2) + (total + edge) + ahead(triple, 2)
        means = total * scale
        ratio = x[REACH : REACH + STEP] / means
        span = pl.ds(at - first, STEP)
        means_ref[span] = means
        ratio_ref[span] = ratio
        send_ref[span] = ratio.astype(BF16)

    row = lax.broadcasted_iota(jnp.int32, shape, 0)
    inner = col_scale * (1.0 / (2 * REACH + 1))
    for at in range(first, last, STEP):
        outer = at in (0, rows - STEP)
        scale = col_scale / counted(row + at, rows).astype(F32) if outer else inner
        box(at, scale)


def add_kernel(ratio_ref, came_ref, sum_ref, send_ref):
    def part(at):
        span = pl.ds(at, STEP)
        total = ratio_ref[span] + came_ref[span].astype(F32)
        sum_ref[span] = total
        send_ref[span] = total.astype(BF16)

    rows_loop(sum_ref.shape[0], part, unroll=True)


def scale_kernel(dates, start, means_ref, sum_ref, came_ref, *refs):
    out_hbm, out, sems = refs[-3:]
    rows = sum_ref.shape[0]
    ends = (0, rows // (2 * STEP) * STEP, rows)

    def copy(piece):
        here = pl.ds(ends[piece], ends[piece + 1] - ends[piece])
        there = pl.ds(start + ends[piece], ends[piece + 1] - ends[piece])
        return pltpu.make_async_copy(out.at[here], out_hbm.at[there], sems.at[piece])

    for piece in range(2):
        for at in range(ends[piece], ends[piece + 1], STEP):
            span = pl.ds(at, STEP)
            total = (sum_ref[span] + came_ref[span].astype(F32)) * (1.0 / dates)
            out[span] = (means_ref[span] * total).astype(BF16)
        copy(piece).start()
    for piece in range(2):
        copy(piece).wait()


def call(kernel, outs, ins, specs=None, mib=8, scratch=(), out_specs=None, aliases=None):
    return pl.pallas_call(
        kernel,
        out_shape=outs,
        in_specs=specs or [VMEM] * len(ins),
        out_specs=out_specs or jax.tree.map(lambda _: VMEM, outs),
        scratch_shapes=scratch,
        input_output_aliases=aliases or {},
        compiler_params=pltpu.CompilerParams(vmem_limit_bytes=mib << 20),
    )(*ins)


def permute(array, axes, pairs):
    return lax.ppermute(array, axes, pairs)


def per_device(tiles, dates, swaths, patch, lead, floor):
    chips = tiles // 2
    relay = chips == 4
    pols = swaths.shape[3]
    swaths, floor = pack(swaths[0]), pack(floor[0])
    blocks = swaths.shape[0]
    rows, subs, _ = floor.shape
    full = (rows, subs, LANES)
    wide = jax.ShapeDtypeStruct(full, F32)
    thin = jax.ShapeDtypeStruct(full, BF16)

    early = 3 if relay else 1
    slots = [s for s in range(chips) if s != early]
    cut = rows * CUT // 16 // STEP * STEP
    pieces = (cut + STEP, rows - cut - STEP) if relay else (rows,)
    starts = (0, cut + STEP)
    piece_shapes = tuple(jax.ShapeDtypeStruct((size, subs, LANES), BF16) for size in pieces)
    canvases = 4 * rows * subs * LANES * chips
    canvas_shape = jax.ShapeDtypeStruct((chips,) + full, F32)
    early_out, acc, own = call(
        functools.partial(place_kernel, relay, chips, early),
        (piece_shapes[0], canvas_shape, canvas_shape),
        tuple(pltpu.with_memory_space_constraint(a, pltpu.HBM) for a in (patch[:, 0], lead, swaths)),
        specs=[HBM] * 3,
        mib=(2 * canvases >> 20) + 4,
        scratch=[
            pltpu.VMEM(swaths.shape, BF16),
            pltpu.SMEM((blocks,), jnp.int32),
            pltpu.SMEM((blocks,), jnp.int32),
            pltpu.SemaphoreType.DMA((blocks + 2,)),
        ],
    )
    partner = [(t, t ^ 1) for t in range(tiles)]
    came_early = permute(early_out, "tile", partner)
    rest = call(
        functools.partial(round_kernel, slots, early),
        jax.ShapeDtypeStruct((chips * rows - pieces[0], subs, LANES), BF16),
        (acc,),
        mib=(2 * canvases >> 20) + 4,
    )
    came = permute(rest, "tile", partner)
    early_send = call(functools.partial(merge_early_kernel, early), piece_shapes[0], (own, came_early))

    def along(array, moves):
        return permute(array, "tile", [(2 * a + core, 2 * b + core) for a, b in moves for core in range(2)])

    shift = 1 if relay else early
    first_pass = [(c, c ^ shift if relay else (c + shift) % chips) for c in range(chips)]
    passing = [along(early_send, first_pass)]
    if relay:
        split = (2, 1, 1)
        outs = piece_shapes + (thin, piece_shapes[1])
    else:
        split = (1,) * (chips - 2)
        outs = (thin,) * (chips - 2)
    keep, *sends = call(
        functools.partial(merge_kernel, slots, early, split),
        (wide,) + outs,
        (own, floor, came),
        mib=(2 * canvases >> 20) + 4,
    )
    if relay:
        *near_sends, far_send, late_send = sends
        passing.append(along(late_send, first_pass))
        far, near = [], []
        for i, passed in enumerate(passing):
            send = call(functools.partial(relay_kernel, starts[i]), piece_shapes[i], (far_send, passed))
            far.append(along(send, [(c, c ^ 2) for c in range(chips)]))
            near.append(along(near_sends[i], [(c, c ^ 1) for c in range(chips)]))
        arrived = [far, near]
    else:
        arrived = [passing]
        for shift, send in zip(slots[1:], sends):
            arrived.append([along(send, [(c, (c + shift) % chips) for c in range(chips)])])

    bits = [1 << b for b in range(dates.bit_length() - 1)]

    def across(step, part):
        pairs = []
        for d in range(dates):
            for t in range(tiles):
                bit = bits[-1 - step] if (t + part) % 2 else bits[step]
                pairs.append((d * tiles + t, (d ^ bit) * tiles + t))
        return pairs

    out = None
    for part, (first, last) in enumerate(((0, cut), (cut, rows))):
        shape = (last - first, subs, LANES)
        wide_part, thin_part = jax.ShapeDtypeStruct(shape, F32), jax.ShapeDtypeStruct(shape, BF16)
        used = [group[: 1 if last + STEP <= pieces[0] else None] for group in arrived]
        means, total, send = call(
            functools.partial(box_kernel, tuple(map(len, used)), pols, first, last),
            (wide_part, wide_part, thin_part),
            (keep, *(piece for group in used for piece in group)),
            mib=8 if relay else 16,
            scratch=[pltpu.VMEM((last - first + 2 * STEP, subs, LANES), F32)],
        )
        for step in range(len(bits)):
            came = permute(send, ("date", "tile"), across(step, part))
            if step + 1 < len(bits):
                total, send = call(add_kernel, (wide_part, thin_part), (total, came), mib=4)
        ins = (means, total, came) + (() if out is None else (out,))
        out = call(
            functools.partial(scale_kernel, float(dates), first),
            thin,
            ins,
            specs=[VMEM] * 3 + [HBM] * (len(ins) - 3),
            out_specs=HBM,
            aliases={3: 0} if len(ins) > 3 else {},
            mib=4,
            scratch=[pltpu.VMEM(shape, BF16), pltpu.SemaphoreType.DMA((2,))],
        )
    return unpack(out, pols)[None]


def device_step(tiles, dates, *arrays):
    return per_device(tiles, dates, *arrays)


def solution(mesh):
    return jax.shard_map(
        functools.partial(device_step, mesh.shape["tile"], mesh.shape["date"]),
        mesh=mesh,
        in_specs=(
            P("date", "tile", None, None, None),
            P("tile", None),
            P("tile"),
            P("date", "tile", None, None),
        ),
        out_specs=P("date", "tile", None, None),
        check_vma=False,
    )
```

```python
import functools

import jax
import jax.numpy as jnp
from jax import lax
from jax.experimental import pallas as pl
from jax.experimental.pallas import tpu as pltpu
from jax.sharding import PartitionSpec as P


LANES = 128
REACH = 3
STEP = 8
CUT = 8
VMEM = pl.BlockSpec(memory_space=pltpu.VMEM)
HBM = pl.BlockSpec(memory_space=pltpu.HBM)
F32, BF16 = jnp.float32, jnp.bfloat16


def pack(array):
    *lead, pols, cols = array.shape
    axis = len(lead)
    array = array.reshape(*lead, pols, cols // LANES, LANES)
    return jnp.swapaxes(array, axis, axis + 1).reshape(*lead, pols * cols // LANES, LANES)


def unpack(array, pols):
    *lead, subs, _ = array.shape
    axis = len(lead)
    array = array.reshape(*lead, subs // pols, pols, LANES)
    return jnp.swapaxes(array, axis, axis + 1).reshape(*lead, pols, subs // pols * LANES)


def rows_loop(count, body, unroll=1):
    lax.fori_loop(0, count // STEP, lambda i, c: (body(pl.multiple_of(i * STEP, STEP)), c)[1], 0, unroll=unroll)


def slot_of(relay, chips, owner_chip, chip):
    return owner_chip ^ chip if relay else lax.rem(owner_chip - chip + chips, chips)


def place_kernel(relay, chips, early, owner_hbm, lead_hbm, swath_hbm, *refs):
    early_ref, acc, own_ref, swath, owner, lead, sems = refs
    blocks, scan, _, _ = swath.shape
    rows = own_ref.shape[1]
    me = lax.axis_index("tile")
    core, chip = me % 2, me // 2
    small = (
        pltpu.make_async_copy(owner_hbm, owner, sems.at[blocks]),
        pltpu.make_async_copy(lead_hbm, lead, sems.at[blocks + 1]),
    )
    for copy in small:
        copy.start()

    def fetch(block):
        return pltpu.make_async_copy(swath_hbm.at[block], swath.at[block], sems.at[block])

    for block in range(blocks):
        fetch(block).start()

    def clear(at):
        zero = jnp.zeros((STEP,) + acc.shape[2:], F32)
        for slot in range(chips):
            acc[slot, pl.ds(at, STEP)] = zero
            own_ref[slot, pl.ds(at, STEP)] = zero

    rows_loop(rows, clear)
    for copy in small:
        copy.wait()

    def add_into(ref, slot, block, base):
        for row in range(0, scan, STEP):
            span = pl.ds(base + row, STEP)
            ref[slot, span] = ref[slot, span] + swath[block, pl.ds(row, STEP)].astype(F32)

    def insert(block, carry):
        target = owner[block]
        base = lead[block]
        slot = slot_of(relay, chips, target // 2, chip)
        fetch(block).wait()

        @pl.when(target % 2 == core)
        def _():
            add_into(own_ref, slot, block, base)

        @pl.when(target % 2 != core)
        def _():
            add_into(acc, slot, block, base)

        return carry

    lax.fori_loop(0, blocks, insert, 0)
    for at in range(0, early_ref.shape[0], STEP):
        early_ref[pl.ds(at, STEP)] = acc[early, pl.ds(at, STEP)].astype(BF16)


def round_kernel(slots, early, acc, rest_ref):
    rows = acc.shape[1]

    def part(at):
        for place, slot in enumerate(slots):
            rest_ref[pl.ds(place * rows + at, STEP)] = acc[slot, pl.ds(at, STEP)].astype(BF16)

    rows_loop(rows, part)
    base = len(slots) * rows
    skipped = rows - (rest_ref.shape[0] - base)
    for at in range(skipped, rows, STEP):
        rest_ref[pl.ds(base + at - skipped, STEP)] = acc[early, pl.ds(at, STEP)].astype(BF16)


def store_rows(refs, at, value):
    for ref in refs:
        if at < ref.shape[0]:
            ref[pl.ds(at, STEP)] = value.astype(ref.dtype)
            return
        at -= ref.shape[0]


def load_rows(refs, at):
    for ref in refs:
        if at < ref.shape[0]:
            return ref[pl.ds(at, STEP)].astype(F32)
        at -= ref.shape[0]


def merge_early_kernel(early, own_ref, came_ref, send_ref):
    for at in range(0, send_ref.shape[0], STEP):
        span = pl.ds(at, STEP)
        send_ref[span] = (own_ref[early, span] + came_ref[span].astype(F32)).astype(BF16)


def merge_kernel(slots, early, pieces, own_ref, floor_ref, came_ref, keep_ref, *send_refs):
    send_refs = iter(send_refs)
    sends = [[next(send_refs) for _ in range(count)] for count in pieces]
    rows = keep_ref.shape[0]
    base = len(slots) * rows
    skipped = rows - (came_ref.shape[0] - base)
    for at in range(0, rows, STEP):
        span = pl.ds(at, STEP)
        if at >= skipped:
            total = own_ref[early, span] + came_ref[pl.ds(base + at - skipped, STEP)].astype(F32)
            sends[-1][0][pl.ds(at - skipped, STEP)] = total.astype(BF16)
        for place, slot in enumerate(slots):
            total = own_ref[slot, span] + came_ref[pl.ds(place * rows + at, STEP)].astype(F32)
            if place:
                store_rows(sends[place - 1], at, total)
            else:
                keep_ref[span] = total + floor_ref[span]


def relay_kernel(start, mine_ref, passing_ref, send_ref):
    for at in range(0, send_ref.shape[0], STEP):
        span = pl.ds(at, STEP)
        total = mine_ref[pl.ds(start + at, STEP)].astype(F32) + passing_ref[span].astype(F32)
        send_ref[span] = total.astype(BF16)


def box_kernel(pieces, pols, first, last, keep_ref, *refs):
    *came_refs, means_ref, send_ref, canvas = refs
    rows, subs, _ = keep_ref.shape
    low, high = max(first - STEP, 0), min(last + STEP, rows)
    origin = first - STEP
    zero = jnp.zeros((STEP, subs, LANES), F32)
    came = iter(came_refs)
    groups = [[next(came) for _ in range(count)] for count in pieces]
    for at in range(origin, last + STEP, STEP):
        total = zero
        if low <= at < high:
            total = keep_ref[pl.ds(at, STEP)]
            for group in groups:
                total = total + load_rows(group, at)
        canvas[pl.ds(at - origin, STEP)] = total

    shape = (STEP, subs, LANES)
    sub = lax.broadcasted_iota(jnp.int32, shape, 1)
    lane = lax.broadcasted_iota(jnp.int32, shape, 2)
    cols = subs // pols * LANES

    def counted(place, length):
        return jnp.minimum(place + REACH, length - 1) - jnp.maximum(place - REACH, 0) + 1

    col_scale = 1.0 / counted(sub // pols * LANES + lane, cols).astype(F32)

    def ahead(x, by):
        after = jnp.where(sub < subs - pols, pltpu.roll(x, subs - pols, 1), 0.0)
        return pltpu.roll(jnp.where(lane < by, after, x), LANES - by, 2)

    def behind(x, by):
        before = jnp.where(sub >= pols, pltpu.roll(x, pols, 1), 0.0)
        return pltpu.roll(jnp.where(lane >= LANES - by, before, x), by, 2)

    edge_ahead = (sub >= subs - pols) & (lane == LANES - 2)
    edge_behind = (sub < pols) & (lane == 1)

    def box(at, scale):
        x = canvas[pl.ds(at - origin - REACH, STEP + 2 * REACH)]
        two = x[:-1] + x[1:]
        four = two[:-2] + two[2:]
        total = four[:STEP] + two[4 : 4 + STEP] + x[6 : 6 + STEP]
        right, left = ahead(total, 1), behind(total, 1)
        triple = left + total + right
        edge = jnp.where(edge_ahead, right, jnp.where(edge_behind, left, 0.0))
        total = behind(triple, 2) + (total + edge) + ahead(triple, 2)
        means = total * scale
        ratio = x[REACH : REACH + STEP] / means
        span = pl.ds(at - first, STEP)
        means_ref[span] = means
        send_ref[span] = ratio.astype(BF16)

    row = lax.broadcasted_iota(jnp.int32, shape, 0)
    inner = col_scale * (1.0 / (2 * REACH + 1))
    for at in range(first, last, STEP):
        outer = at in (0, rows - STEP)
        scale = col_scale / counted(row + at, rows).astype(F32) if outer else inner
        box(at, scale)


def add_kernel(ratio_ref, came_ref, sum_ref, send_ref):
    def part(at):
        span = pl.ds(at, STEP)
        total = ratio_ref[span].astype(F32) + came_ref[span].astype(F32)
        sum_ref[span] = total
        send_ref[span] = total.astype(BF16)

    rows_loop(sum_ref.shape[0], part, unroll=True)


def scale_kernel(dates, start, means_ref, sum_ref, came_ref, *refs):
    out_hbm, out, sems = refs[-3:]
    rows = sum_ref.shape[0]
    ends = (0, rows // (2 * STEP) * STEP, rows)

    def copy(piece):
        here = pl.ds(ends[piece], ends[piece + 1] - ends[piece])
        there = pl.ds(start + ends[piece], ends[piece + 1] - ends[piece])
        return pltpu.make_async_copy(out.at[here], out_hbm.at[there], sems.at[piece])

    for piece in range(2):
        for at in range(ends[piece], ends[piece + 1], STEP):
            span = pl.ds(at, STEP)
            total = (sum_ref[span].astype(F32) + came_ref[span].astype(F32)) * (1.0 / dates)
            out[span] = (means_ref[span] * total).astype(BF16)
        copy(piece).start()
    for piece in range(2):
        copy(piece).wait()


def call(kernel, outs, ins, specs=None, mib=8, scratch=(), out_specs=None, aliases=None):
    return pl.pallas_call(
        kernel,
        out_shape=outs,
        in_specs=specs or [VMEM] * len(ins),
        out_specs=out_specs or jax.tree.map(lambda _: VMEM, outs),
        scratch_shapes=scratch,
        input_output_aliases=aliases or {},
        compiler_params=pltpu.CompilerParams(vmem_limit_bytes=mib << 20),
    )(*ins)


def permute(array, axes, pairs):
    return lax.ppermute(array, axes, pairs)


def per_device(tiles, dates, swaths, patch, lead, floor):
    chips = tiles // 2
    relay = chips == 4
    pols = swaths.shape[3]
    swaths, floor = pack(swaths[0]), pack(floor[0])
    blocks = swaths.shape[0]
    rows, subs, _ = floor.shape
    full = (rows, subs, LANES)
    wide = jax.ShapeDtypeStruct(full, F32)
    thin = jax.ShapeDtypeStruct(full, BF16)

    early = 3 if relay else 1
    slots = [s for s in range(chips) if s != early]
    cut = rows * CUT // 16 // STEP * STEP
    pieces = (cut + STEP, rows - cut - STEP) if relay else (rows,)
    starts = (0, cut + STEP)
    piece_shapes = tuple(jax.ShapeDtypeStruct((size, subs, LANES), BF16) for size in pieces)
    canvases = 4 * rows * subs * LANES * chips
    canvas_shape = jax.ShapeDtypeStruct((chips,) + full, F32)
    early_out, acc, own = call(
        functools.partial(place_kernel, relay, chips, early),
        (piece_shapes[0], canvas_shape, canvas_shape),
        tuple(pltpu.with_memory_space_constraint(a, pltpu.HBM) for a in (patch[:, 0], lead, swaths)),
        specs=[HBM] * 3,
        mib=(2 * canvases >> 20) + 4,
        scratch=[
            pltpu.VMEM(swaths.shape, BF16),
            pltpu.SMEM((blocks,), jnp.int32),
            pltpu.SMEM((blocks,), jnp.int32),
            pltpu.SemaphoreType.DMA((blocks + 2,)),
        ],
    )
    partner = [(t, t ^ 1) for t in range(tiles)]
    came_early = permute(early_out, "tile", partner)
    rest = call(
        functools.partial(round_kernel, slots, early),
        jax.ShapeDtypeStruct((chips * rows - pieces[0], subs, LANES), BF16),
        (acc,),
        mib=(2 * canvases >> 20) + 4,
    )
    came = permute(rest, "tile", partner)
    early_send = call(functools.partial(merge_early_kernel, early), piece_shapes[0], (own, came_early))

    def along(array, moves):
        return permute(array, "tile", [(2 * a + core, 2 * b + core) for a, b in moves for core in range(2)])

    shift = 1 if relay else early
    first_pass = [(c, c ^ shift if relay else (c + shift) % chips) for c in range(chips)]
    passing = [along(early_send, first_pass)]
    if relay:
        split = (2, 1, 1)
        outs = piece_shapes + (thin, piece_shapes[1])
    else:
        split = (1,) * (chips - 2)
        outs = (thin,) * (chips - 2)
    keep, *sends = call(
        functools.partial(merge_kernel, slots, early, split),
        (wide,) + outs,
        (own, floor, came),
        mib=(2 * canvases >> 20) + 4,
    )
    if relay:
        *near_sends, far_send, late_send = sends
        passing.append(along(late_send, first_pass))
        far, near = [], []
        for i, passed in enumerate(passing):
            send = call(functools.partial(relay_kernel, starts[i]), piece_shapes[i], (far_send, passed))
            far.append(along(send, [(c, c ^ 2) for c in range(chips)]))
            near.append(along(near_sends[i], [(c, c ^ 1) for c in range(chips)]))
        arrived = [far, near]
    else:
        arrived = [passing]
        for shift, send in zip(slots[1:], sends):
            arrived.append([along(send, [(c, (c + shift) % chips) for c in range(chips)])])

    bits = [1 << b for b in range(dates.bit_length() - 1)]

    out = None
    for first, last in ((0, cut), (cut, rows)):
        shape = (last - first, subs, LANES)
        wide_part, thin_part = jax.ShapeDtypeStruct(shape, F32), jax.ShapeDtypeStruct(shape, BF16)
        used = [group[: 1 if last + STEP <= pieces[0] else None] for group in arrived]
        means, send = call(
            functools.partial(box_kernel, tuple(map(len, used)), pols, first, last),
            (wide_part, thin_part),
            (keep, *(piece for group in used for piece in group)),
            mib=8 if relay else 16,
            scratch=[pltpu.VMEM((last - first + 2 * STEP, subs, LANES), F32)],
        )
        total = send
        for step, bit in enumerate(bits):
            came = permute(send, "date", [(d, d ^ bit) for d in range(dates)])
            if step + 1 < len(bits):
                total, send = call(add_kernel, (wide_part, thin_part), (total, came), mib=4)
        ins = (means, total, came) + (() if out is None else (out,))
        out = call(
            functools.partial(scale_kernel, float(dates), first),
            thin,
            ins,
            specs=[VMEM] * 3 + [HBM] * (len(ins) - 3),
            out_specs=HBM,
            aliases={3: 0} if len(ins) > 3 else {},
            mib=4,
            scratch=[pltpu.VMEM(shape, BF16), pltpu.SemaphoreType.DMA((2,))],
        )
    return unpack(out, pols)[None]


def device_step(tiles, dates, *arrays):
    return per_device(tiles, dates, *arrays)


def solution(mesh):
    return jax.shard_map(
        functools.partial(device_step, mesh.shape["tile"], mesh.shape["date"]),
        mesh=mesh,
        in_specs=(
            P("date", "tile", None, None, None),
            P("tile", None),
            P("tile"),
            P("date", "tile", None, None),
        ),
        out_specs=P("date", "tile", None, None),
        check_vma=False,
    )
```

```python
import functools

import jax
import jax.numpy as jnp
from jax import lax
from jax.experimental import pallas as pl
from jax.experimental.pallas import tpu as pltpu
from jax.sharding import PartitionSpec as P


LANES = 128
REACH = 3
STEP = 8
CUT = 8
VMEM = pl.BlockSpec(memory_space=pltpu.VMEM)
HBM = pl.BlockSpec(memory_space=pltpu.HBM)
F32, BF16 = jnp.float32, jnp.bfloat16


def pack(array):
    *lead, pols, cols = array.shape
    axis = len(lead)
    array = array.reshape(*lead, pols, cols // LANES, LANES)
    return jnp.swapaxes(array, axis, axis + 1).reshape(*lead, pols * cols // LANES, LANES)


def unpack(array, pols):
    *lead, subs, _ = array.shape
    axis = len(lead)
    array = array.reshape(*lead, subs // pols, pols, LANES)
    return jnp.swapaxes(array, axis, axis + 1).reshape(*lead, pols, subs // pols * LANES)


def rows_loop(count, body, unroll=1):
    lax.fori_loop(0, count // STEP, lambda i, c: (body(pl.multiple_of(i * STEP, STEP)), c)[1], 0, unroll=unroll)


def slot_of(relay, chips, owner_chip, chip):
    return owner_chip ^ chip if relay else lax.rem(owner_chip - chip + chips, chips)


def place_kernel(relay, chips, early, owner_hbm, lead_hbm, swath_hbm, *refs):
    early_ref, acc, own_ref, swath, owner, lead, sems = refs
    blocks, scan, _, _ = swath.shape
    rows = own_ref.shape[1]
    me = lax.axis_index("tile")
    core, chip = me % 2, me // 2
    small = (
        pltpu.make_async_copy(owner_hbm, owner, sems.at[blocks]),
        pltpu.make_async_copy(lead_hbm, lead, sems.at[blocks + 1]),
    )
    for copy in small:
        copy.start()

    def fetch(block):
        return pltpu.make_async_copy(swath_hbm.at[block], swath.at[block], sems.at[block])

    for block in range(blocks):
        fetch(block).start()

    def clear(at):
        zero = jnp.zeros((STEP,) + acc.shape[2:], F32)
        for slot in range(chips):
            acc[slot, pl.ds(at, STEP)] = zero
            own_ref[slot, pl.ds(at, STEP)] = zero

    rows_loop(rows, clear)
    for copy in small:
        copy.wait()

    def add_into(ref, slot, block, base):
        for row in range(0, scan, STEP):
            span = pl.ds(base + row, STEP)
            ref[slot, span] = ref[slot, span] + swath[block, pl.ds(row, STEP)].astype(F32)

    def insert(block, carry):
        target = owner[block]
        base = lead[block]
        slot = slot_of(relay, chips, target // 2, chip)
        fetch(block).wait()

        @pl.when(target % 2 == core)
        def _():
            add_into(own_ref, slot, block, base)

        @pl.when(target % 2 != core)
        def _():
            add_into(acc, slot, block, base)

        return carry

    lax.fori_loop(0, blocks, insert, 0)
    for at in range(0, early_ref.shape[0], STEP):
        early_ref[pl.ds(at, STEP)] = acc[early, pl.ds(at, STEP)].astype(BF16)


def round_kernel(slots, early, acc, rest_ref):
    rows = acc.shape[1]

    def part(at):
        for place, slot in enumerate(slots):
            rest_ref[pl.ds(place * rows + at, STEP)] = acc[slot, pl.ds(at, STEP)].astype(BF16)

    rows_loop(rows, part)
    base = len(slots) * rows
    skipped = rows - (rest_ref.shape[0] - base)
    for at in range(skipped, rows, STEP):
        rest_ref[pl.ds(base + at - skipped, STEP)] = acc[early, pl.ds(at, STEP)].astype(BF16)


def store_rows(refs, at, value):
    for ref in refs:
        if at < ref.shape[0]:
            ref[pl.ds(at, STEP)] = value.astype(ref.dtype)
            return
        at -= ref.shape[0]


def load_rows(refs, at):
    for ref in refs:
        if at < ref.shape[0]:
            return ref[pl.ds(at, STEP)].astype(F32)
        at -= ref.shape[0]


def merge_early_kernel(early, own_ref, came_ref, send_ref):
    for at in range(0, send_ref.shape[0], STEP):
        span = pl.ds(at, STEP)
        send_ref[span] = (own_ref[early, span] + came_ref[span].astype(F32)).astype(BF16)


def merge_kernel(slots, early, pieces, own_ref, floor_ref, came_ref, keep_ref, *send_refs):
    send_refs = iter(send_refs)
    sends = [[next(send_refs) for _ in range(count)] for count in pieces]
    rows = keep_ref.shape[0]
    base = len(slots) * rows
    skipped = rows - (came_ref.shape[0] - base)
    for at in range(0, rows, STEP):
        span = pl.ds(at, STEP)
        if at >= skipped:
            total = own_ref[early, span] + came_ref[pl.ds(base + at - skipped, STEP)].astype(F32)
            sends[-1][0][pl.ds(at - skipped, STEP)] = total.astype(BF16)
        for place, slot in enumerate(slots):
            total = own_ref[slot, span] + came_ref[pl.ds(place * rows + at, STEP)].astype(F32)
            if place:
                store_rows(sends[place - 1], at, total)
            else:
                keep_ref[span] = total + floor_ref[span]


def relay_kernel(start, mine_ref, passing_ref, send_ref):
    for at in range(0, send_ref.shape[0], STEP):
        span = pl.ds(at, STEP)
        total = mine_ref[pl.ds(start + at, STEP)].astype(F32) + passing_ref[span].astype(F32)
        send_ref[span] = total.astype(BF16)


def box_kernel(pieces, pols, first, last, keep_ref, *refs):
    *came_refs, means_ref, ratio_ref, send_ref, canvas = refs
    rows, subs, _ = keep_ref.shape
    low, high = max(first - STEP, 0), min(last + STEP, rows)
    origin = first - STEP
    zero = jnp.zeros((STEP, subs, LANES), F32)
    came = iter(came_refs)
    groups = [[next(came) for _ in range(count)] for count in pieces]
    for at in range(origin, last + STEP, STEP):
        total = zero
        if low <= at < high:
            total = keep_ref[pl.ds(at, STEP)]
            for group in groups:
                total = total + load_rows(group, at)
        canvas[pl.ds(at - origin, STEP)] = total

    shape = (STEP, subs, LANES)
    sub = lax.broadcasted_iota(jnp.int32, shape, 1)
    lane = lax.broadcasted_iota(jnp.int32, shape, 2)
    cols = subs // pols * LANES

    def counted(place, length):
        return jnp.minimum(place + REACH, length - 1) - jnp.maximum(place - REACH, 0) + 1

    col_scale = 1.0 / counted(sub // pols * LANES + lane, cols).astype(F32)

    def ahead(x, by):
        after = jnp.where(sub < subs - pols, pltpu.roll(x, subs - pols, 1), 0.0)
        return pltpu.roll(jnp.where(lane < by, after, x), LANES - by, 2)

    def behind(x, by):
        before = jnp.where(sub >= pols, pltpu.roll(x, pols, 1), 0.0)
        return pltpu.roll(jnp.where(lane >= LANES - by, before, x), by, 2)

    edge_ahead = (sub >= subs - pols) & (lane == LANES - 2)
    edge_behind = (sub < pols) & (lane == 1)

    def box(at, scale):
        x = canvas[pl.ds(at - origin - REACH, STEP + 2 * REACH)]
        two = x[:-1] + x[1:]
        four = two[:-2] + two[2:]
        total = four[:STEP] + two[4 : 4 + STEP] + x[6 : 6 + STEP]
        right, left = ahead(total, 1), behind(total, 1)
        triple = left + total + right
        edge = jnp.where(edge_ahead, right, jnp.where(edge_behind, left, 0.0))
        total = behind(triple, 2) + (total + edge) + ahead(triple, 2)
        means = total * scale
        ratio = x[REACH : REACH + STEP] / means
        span = pl.ds(at - first, STEP)
        means_ref[span] = means
        ratio_ref[span] = ratio
        send_ref[span] = ratio.astype(BF16)

    row = lax.broadcasted_iota(jnp.int32, shape, 0)
    inner = col_scale * (1.0 / (2 * REACH + 1))
    for at in range(first, last, STEP):
        outer = at in (0, rows - STEP)
        scale = col_scale / counted(row + at, rows).astype(F32) if outer else inner
        box(at, scale)


def add_kernel(ratio_ref, came_ref, sum_ref, send_ref):
    def part(at):
        span = pl.ds(at, STEP)
        total = ratio_ref[span] + came_ref[span].astype(F32)
        sum_ref[span] = total
        send_ref[span] = total.astype(BF16)

    rows_loop(sum_ref.shape[0], part, unroll=True)


def scale_kernel(dates, start, means_ref, sum_ref, came_ref, *refs):
    out_hbm, out, sems = refs[-3:]
    rows = sum_ref.shape[0]
    ends = (0, rows // (2 * STEP) * STEP, rows)

    def copy(piece):
        here = pl.ds(ends[piece], ends[piece + 1] - ends[piece])
        there = pl.ds(start + ends[piece], ends[piece + 1] - ends[piece])
        return pltpu.make_async_copy(out.at[here], out_hbm.at[there], sems.at[piece])

    for piece in range(2):
        for at in range(ends[piece], ends[piece + 1], STEP):
            span = pl.ds(at, STEP)
            total = (sum_ref[span] + came_ref[span].astype(F32)) * (1.0 / dates)
            out[span] = (means_ref[span] * total).astype(BF16)
        copy(piece).start()
    for piece in range(2):
        copy(piece).wait()


def call(kernel, outs, ins, specs=None, mib=8, scratch=(), out_specs=None, aliases=None):
    return pl.pallas_call(
        kernel,
        out_shape=outs,
        in_specs=specs or [VMEM] * len(ins),
        out_specs=out_specs or jax.tree.map(lambda _: VMEM, outs),
        scratch_shapes=scratch,
        input_output_aliases=aliases or {},
        compiler_params=pltpu.CompilerParams(vmem_limit_bytes=mib << 20),
    )(*ins)


def permute(array, axes, pairs):
    return lax.ppermute(array, axes, pairs)


def per_device(tiles, dates, swaths, patch, lead, floor):
    chips = tiles // 2
    relay = chips == 4
    pols = swaths.shape[3]
    swaths, floor = pack(swaths[0]), pack(floor[0])
    blocks = swaths.shape[0]
    rows, subs, _ = floor.shape
    full = (rows, subs, LANES)
    wide = jax.ShapeDtypeStruct(full, F32)
    thin = jax.ShapeDtypeStruct(full, BF16)

    early = 3 if relay else 1
    slots = [s for s in range(chips) if s != early]
    cut = rows * CUT // 16 // STEP * STEP
    pieces = (cut + STEP, rows - cut - STEP) if relay else (rows,)
    starts = (0, cut + STEP)
    piece_shapes = tuple(jax.ShapeDtypeStruct((size, subs, LANES), BF16) for size in pieces)
    canvases = 4 * rows * subs * LANES * chips
    canvas_shape = jax.ShapeDtypeStruct((chips,) + full, F32)
    early_out, acc, own = call(
        functools.partial(place_kernel, relay, chips, early),
        (piece_shapes[0], canvas_shape, canvas_shape),
        tuple(pltpu.with_memory_space_constraint(a, pltpu.HBM) for a in (patch[:, 0], lead, swaths)),
        specs=[HBM] * 3,
        mib=(2 * canvases >> 20) + 4,
        scratch=[
            pltpu.VMEM(swaths.shape, BF16),
            pltpu.SMEM((blocks,), jnp.int32),
            pltpu.SMEM((blocks,), jnp.int32),
            pltpu.SemaphoreType.DMA((blocks + 2,)),
        ],
    )
    partner = [(t, t ^ 1) for t in range(tiles)]
    came_early = permute(early_out, "tile", partner)
    rest = call(
        functools.partial(round_kernel, slots, early),
        jax.ShapeDtypeStruct((chips * rows - pieces[0], subs, LANES), BF16),
        (acc,),
        mib=(2 * canvases >> 20) + 4,
    )
    came = permute(rest, "tile", partner)
    early_send = call(functools.partial(merge_early_kernel, early), piece_shapes[0], (own, came_early))

    def along(array, moves):
        return permute(array, "tile", [(2 * a + core, 2 * b + core) for a, b in moves for core in range(2)])

    shift = 1 if relay else early
    first_pass = [(c, c ^ shift if relay else (c + shift) % chips) for c in range(chips)]
    passing = [along(early_send, first_pass)]
    if relay:
        split = (2, 1, 1)
        outs = piece_shapes + (thin, piece_shapes[1])
    else:
        split = (1,) * (chips - 2)
        outs = (thin,) * (chips - 2)
    keep, *sends = call(
        functools.partial(merge_kernel, slots, early, split),
        (wide,) + outs,
        (own, floor, came),
        mib=(2 * canvases >> 20) + 4,
    )
    if relay:
        *near_sends, far_send, late_send = sends
        passing.append(along(late_send, first_pass))
        far, near = [], []
        for i, passed in enumerate(passing):
            send = call(functools.partial(relay_kernel, starts[i]), piece_shapes[i], (far_send, passed))
            far.append(along(send, [(c, c ^ 2) for c in range(chips)]))
            near.append(along(near_sends[i], [(c, c ^ 1) for c in range(chips)]))
        arrived = [far, near]
    else:
        arrived = [passing]
        for shift, send in zip(slots[1:], sends):
            arrived.append([along(send, [(c, (c + shift) % chips) for c in range(chips)])])

    bits = [1 << b for b in range(dates.bit_length() - 1)][::-1]

    out = None
    for first, last in ((0, cut), (cut, rows)):
        shape = (last - first, subs, LANES)
        wide_part, thin_part = jax.ShapeDtypeStruct(shape, F32), jax.ShapeDtypeStruct(shape, BF16)
        used = [group[: 1 if last + STEP <= pieces[0] else None] for group in arrived]
        means, total, send = call(
            functools.partial(box_kernel, tuple(map(len, used)), pols, first, last),
            (wide_part, wide_part, thin_part),
            (keep, *(piece for group in used for piece in group)),
            mib=8 if relay else 16,
            scratch=[pltpu.VMEM((last - first + 2 * STEP, subs, LANES), F32)],
        )
        for step, bit in enumerate(bits):
            came = permute(send, "date", [(d, d ^ bit) for d in range(dates)])
            if step + 1 < len(bits):
                total, send = call(add_kernel, (wide_part, thin_part), (total, came), mib=4)
        ins = (means, total, came) + (() if out is None else (out,))
        out = call(
            functools.partial(scale_kernel, float(dates), first),
            thin,
            ins,
            specs=[VMEM] * 3 + [HBM] * (len(ins) - 3),
            out_specs=HBM,
            aliases={3: 0} if len(ins) > 3 else {},
            mib=4,
            scratch=[pltpu.VMEM(shape, BF16), pltpu.SemaphoreType.DMA((2,))],
        )
    return unpack(out, pols)[None]


def device_step(tiles, dates, *arrays):
    return per_device(tiles, dates, *arrays)


def solution(mesh):
    return jax.shard_map(
        functools.partial(device_step, mesh.shape["tile"], mesh.shape["date"]),
        mesh=mesh,
        in_specs=(
            P("date", "tile", None, None, None),
            P("tile", None),
            P("tile"),
            P("date", "tile", None, None),
        ),
        out_specs=P("date", "tile", None, None),
        check_vma=False,
    )
```
